128 devices in a mesh: col: 8 (over z, core), ang: 16 (over y, x).
Axes of the slice: x: 4, y: 4, z: 4, core: 2. Of those that a mesh axis runs over, the one named last changes fastest.
Arguments:
- projections: bfloat16 [128, 256, 8192], P('ang', None, 'col'), may hold values from -8 to 24
- detector_offset: float32 [256, 8192], P(None, 'col'), may hold values from -12 to 12
- drift_offsets: int32 [2, 128], replicated, may hold values from -4 to 4
- drift_fractions: int32 [2, 128], replicated, may hold values from 0 to 255
- cycle_widths: int32 [256], P('ang'), may hold values from 1 to 16
Outputs:
- filtered: float32 [128, 256, 8192], P(None, 'ang', 'col')
The draws below stay inside these ranges and needn't reach their ends.
Inputs may be any that keep to these rules, and one draw needn't show every extreme that they name: `drift_offsets`: both rows reach -4 and 4.
All inputs are finite; a program needn't handle non-finite values.
Results may differ from the reference program's by a relative error of at most 0.003.
The reference program's roundings to bfloat16 on the way (of `leveled`, `aligned` and `ramp_taps`) count: a program that leaves them out, or rounds other values in their place, can miss the bound.
Values may be sent and summed in bfloat16 or wider, within the bound.
A program may use at most 128 MiB of HBM per device.

```python
import math
import jax
import jax.numpy as jnp
from jax import lax

W = 8192
DRIFT = 4
BWMAX = 16
RW = 256
ANGLES = 128
ROWS = 256


def draw_projections(key, part):
    feature_count = 48
    keys = jax.random.split(jax.random.fold_in(key, 7), 6)
    centres = jax.random.randint(keys[0], (feature_count,), 0, W)
    spans = jax.random.randint(keys[1], (feature_count,), max(W // 64, 2), max(W // 4, 3))
    speeds = jax.random.randint(keys[2], (feature_count,), -4, 5)
    levels = jax.random.randint(keys[3], (feature_count,), 2, 13)
    angle_index = jnp.arange(ANGLES, dtype=jnp.int32)
    column_index = jnp.arange(W, dtype=jnp.int32)
    travel = speeds[:, None] * angle_index[None, :] * W // (4 * ANGLES)
    starts = (centres[:, None] + travel) % W
    offsets = (column_index[None, None, :] - starts[:, :, None]) % W
    inside = (offsets < spans[:, None, None]).astype(jnp.float32)
    heights = levels.astype(jnp.float32) / 8.0
    profile = jnp.sum(heights[:, None, None] * inside, axis=0)
    base_level = 2.0
    row_gain = jax.random.uniform(keys[4], (ROWS,), jnp.float32, 0.5, 1.5)
    noise = jax.random.normal(keys[5], (ANGLES, ROWS, W), jnp.float32)
    values = (base_level + profile)[:, None, :] * row_gain[None, :, None] + noise
    return jnp.clip(values, -8.0, 24.0).astype(jnp.bfloat16)


def with_ends(entries, rng, least, top_value):
    extent = entries.shape
    index_at = [jax.random.randint(jax.random.fold_in(rng, axis), (), 0, extent[axis]) for axis in range(len(extent))]
    entries = entries.at[tuple(index_at)].set(least)
    longest = extent.index(max(extent))
    index_at[longest] = (index_at[longest] + 1) % extent[longest]
    return entries.at[tuple(index_at)].set(top_value)


def steps_of(key, shape, cuts, least, largest):
    factor_of = 1.0
    for axis_at, blocks in cuts:
        steps = jax.random.uniform(jax.random.fold_in(jax.random.fold_in(key, 6), axis_at), (blocks,), jnp.float32, least / len(cuts), largest / len(cuts))
        factor_of = factor_of * jnp.repeat(jnp.exp(steps), shape[axis_at] // blocks).reshape((-1,) + (1,) * (len(shape) - 1 - axis_at))
    return factor_of


def bell_draw(key, shape, width, limit, shards=(), held_as=jnp.bfloat16):
    array = width * jax.random.normal(key, shape, jnp.float32)
    if shards:
        array = array * steps_of(key, shape, shards, -0.22, 0.18)
    return jnp.clip(array, -limit, limit).astype(held_as)


def setup_inputs(seed: int = 0) -> dict:
    key_list = jax.random.split(jax.random.key(seed), 6)
    projections = draw_projections(jax.random.fold_in(key_list[5], 71), 0)
    detector_offset = bell_draw(key_list[1], (ROWS, W), 2.0, 12.0, ((1, 8),), jnp.float32)
    drift_offsets = with_ends(jax.random.randint(key_list[2], (2, ANGLES), -DRIFT, DRIFT + 1), jax.random.fold_in(key_list[2], 1), -DRIFT, DRIFT).astype(jnp.int32)
    drift_fractions = with_ends(jax.random.randint(key_list[3], (2, ANGLES), 0, 256), jax.random.fold_in(key_list[3], 1), 0, 255).astype(jnp.int32)
    cycle_widths = with_ends(jax.random.randint(key_list[4], (ROWS,), 1, BWMAX + 1), jax.random.fold_in(key_list[4], 1), 1, BWMAX).astype(jnp.int32)
    return {"projections": projections, "detector_offset": detector_offset, "drift_offsets": drift_offsets, "drift_fractions": drift_fractions, "cycle_widths": cycle_widths}


def cubic_weights(fraction):
    scaled = fraction.astype(jnp.float32) / 256.0
    squared = scaled * scaled
    cubed = squared * scaled
    return jnp.stack([(-cubed + 2.0 * squared - scaled) * 0.5, (3.0 * cubed - 5.0 * squared + 2.0) * 0.5, (-3.0 * cubed + 4.0 * squared + scaled) * 0.5, (cubed - squared) * 0.5], axis=-1)


def ramp_value(positions):
    odd_mask = (jnp.abs(positions) % 2) == 1
    safe_value = jnp.where(positions == 0, 1, positions).astype(jnp.float32)
    tap_value = jnp.where(positions == 0, 0.25, jnp.where(odd_mask, -1.0 / (math.pi ** 2 * safe_value * safe_value), 0.0))
    return tap_value.astype(jnp.float32)


def cycle_term(mean_ext, inside_ext, widths, inner_width):
    running = jnp.zeros((mean_ext.shape[0], inner_width), jnp.float32)
    counted = jnp.zeros((mean_ext.shape[0], inner_width), jnp.float32)
    for displacement in range(-BWMAX, BWMAX + 1):
        chosen = (abs(displacement) <= widths).astype(jnp.float32)[:, None]
        running = running + chosen * mean_ext[:, BWMAX + displacement:BWMAX + displacement + inner_width]
        counted = counted + chosen * inside_ext[None, BWMAX + displacement:BWMAX + displacement + inner_width]
    centre = mean_ext[:, BWMAX:BWMAX + inner_width]
    return centre - running / jnp.maximum(counted, 1.0)


def reference(projections, detector_offset, drift_offsets, drift_fractions, cycle_widths):
    margin = DRIFT + 2
    row_weights = cubic_weights(drift_fractions[0])
    col_weights = cubic_weights(drift_fractions[1])

    def single_angle(inputs):
        picture, row_shift, col_shift, vert_taps, horz_taps = inputs
        raw_sum = picture.astype(jnp.float32) + detector_offset
        padded = jnp.pad(raw_sum, ((margin, margin), (0, 0)))
        leveled = jnp.zeros((ROWS, W), jnp.float32)
        for tap_index in range(4):
            leveled = leveled + vert_taps[tap_index] * lax.dynamic_slice_in_dim(padded, margin + row_shift + tap_index - 1, ROWS, 0)
        leveled = lax.optimization_barrier(leveled.astype(jnp.bfloat16))
        padded_cols = jnp.pad(leveled.astype(jnp.float32), ((0, 0), (margin, margin)))
        aligned = jnp.zeros((ROWS, W), jnp.float32)
        for tap_index in range(4):
            aligned = aligned + horz_taps[tap_index] * lax.dynamic_slice_in_dim(padded_cols, margin + col_shift + tap_index - 1, W, 1)
        return aligned.astype(jnp.bfloat16)

    aligned = lax.map(single_angle, (projections, drift_offsets[0], drift_offsets[1], row_weights, col_weights))
    mean_map = jnp.sum(aligned, axis=0, dtype=jnp.float32) / ANGLES
    mean_ext = jnp.pad(mean_map, ((0, 0), (BWMAX, BWMAX)))
    inside_ext = jnp.pad(jnp.ones((W,), jnp.float32), (BWMAX, BWMAX))
    cycle_est = cycle_term(mean_ext, inside_ext, cycle_widths, W)
    ramp_taps = ramp_value(jnp.arange(-RW, RW + 1).astype(jnp.int32))
    ramp_taps = lax.optimization_barrier(ramp_taps.astype(jnp.bfloat16)).astype(jnp.float32)
    fft_len = 2 * W
    kernel = jnp.zeros((fft_len,), jnp.float32)
    kernel = kernel.at[:RW + 1].set(ramp_taps[RW:])
    kernel = kernel.at[fft_len - RW:].set(ramp_taps[:RW])
    kernel_freq = jnp.fft.rfft(kernel)

    def filter_one(picture):
        corrected = picture.astype(jnp.float32) - cycle_est
        padded_rows = jnp.pad(corrected, ((0, 0), (0, fft_len - W)))
        result = jnp.fft.irfft(jnp.fft.rfft(padded_rows, axis=1) * kernel_freq[None, :], n=fft_len, axis=1)[:, :W]
        return result.astype(jnp.float32)

    return lax.map(filter_one, aligned)
```

```python
import functools
import math

import jax
import jax.numpy as jnp
from jax import lax
from jax.experimental import pallas as pl
from jax.experimental.pallas import tpu as pltpu
from jax.sharding import PartitionSpec as P

BWMAX = 16
RW = 256
MESH = pl.DeviceIdType.MESH
F32 = jnp.float32
BF16 = jnp.bfloat16

PARTNERS = (
    (0, 2), (2, 0), (1, 3), (3, 1), (0, 1), (2, 2), (1, 0), (3, 3),
    (0, 3), (1, 2), (3, 0), (2, 1), (1, 1), (2, 3), (3, 2),
)
SIDE = 4
MARGIN = 8
LANES = 128
AHEAD = 2
MEDGE = 384


def cubic_taps(fraction):
    t = fraction.astype(F32) / 256.0
    t2 = t * t
    t3 = t2 * t
    return (
        (-t3 + 2.0 * t2 - t) * 0.5,
        (3.0 * t3 - 5.0 * t2 + 2.0) * 0.5,
        (-3.0 * t3 + 4.0 * t2 + t) * 0.5,
        (t3 - t2) * 0.5,
    )


def ramp_tile(shift):
    rows = lax.broadcasted_iota(jnp.int32, (RW, RW), 0)
    cols = lax.broadcasted_iota(jnp.int32, (RW, RW), 1)
    n = rows - cols + shift
    odd = (n & 1) == 1
    safe = jnp.where(n == 0, 1, n).astype(F32)
    value = jnp.where(n == 0, 0.25, jnp.where(odd, -1.0 / (math.pi**2 * safe * safe), 0.0))
    return jnp.where(jnp.abs(n) <= RW, value, 0.0)


def exchange_kernel(
    proj, offset, doff_in, dfrac_in,
    sino, halo_l, halo_r, mean, ramp,
    pbuf, obuf, doff, dfrac, padded, lev, sent, got, al,
    d_sem, p_sem, o_sem, es_sem, er_sem, own_sem, s_sem, r_sem, hs_sem, hr_sem, ms_sem, mr_sem,
):
    me = lax.axis_index("ang")
    col = lax.axis_index("col")
    n_col = lax.axis_size("col")
    angles, rows, width = proj.shape
    slabs = sino.shape[0]
    slab = rows // slabs
    blocks = width // LANES
    y, x = me // SIDE, lax.rem(me, SIDE)
    sign = 1 - 2 * lax.rem(col, 2)
    left = lax.rem(col + n_col - 1, n_col)
    right = lax.rem(col + 1, n_col)

    def partner(step):
        return lax.rem(y + SIDE + sign * step[0], SIDE) * SIDE + lax.rem(x + SIDE + sign * step[1], SIDE)

    def frame_copy(a):
        return pltpu.make_async_copy(proj.at[a], pbuf.at[a], p_sem.at[a])

    drift_copies = (
        pltpu.make_async_copy(doff_in, doff, d_sem.at[0]),
        pltpu.make_async_copy(dfrac_in, dfrac, d_sem.at[1]),
    )
    for copy in drift_copies:
        copy.start()
    offset_copy = pltpu.make_async_copy(offset, obuf, o_sem)
    frame_copy(0).start()
    offset_copy.start()
    for a in range(1, angles):
        frame_copy(a).start()

    barrier = pltpu.get_barrier_semaphore()
    for step in PARTNERS:
        pl.semaphore_signal(barrier, 1, device_id={"ang": partner(step)}, device_id_type=MESH)
    for neighbour in (left, right):
        pl.semaphore_signal(barrier, 1, device_id={"col": neighbour}, device_id_type=MESH)

    zeros = jnp.zeros((blocks, MARGIN, LANES), F32)
    padded[:, 0:MARGIN, :] = zeros
    padded[:, MARGIN + rows : 2 * MARGIN + rows, :] = zeros

    def edge_copies(a):
        return (
            pltpu.make_async_remote_copy(
                sent.at[a, 1], got.at[a, 0], es_sem.at[a, 0], er_sem.at[a, 0],
                device_id={"col": right}, device_id_type=MESH,
            ),
            pltpu.make_async_remote_copy(
                sent.at[a, 0], got.at[a, 1], es_sem.at[a, 1], er_sem.at[a, 1],
                device_id={"col": left}, device_id_type=MESH,
            ),
        )

    def level(a):
        frame_copy(a).wait()
        shift = doff[0, me * angles + a]
        taps = cubic_taps(dfrac[0, me * angles + a])

        def fill(j, carry):
            at = pl.multiple_of(j * slab, slab)
            for b in range(blocks):
                lanes = pl.ds(b * LANES, LANES)
                padded[b, pl.ds(at + MARGIN, slab), :] = (
                    pbuf[a, pl.ds(at, slab), lanes].astype(F32) + obuf[pl.ds(at, slab), lanes]
                )
            return carry

        lax.fori_loop(0, slabs, fill, 0)

        def mix(j, carry):
            at = pl.multiple_of(j * slab, slab)
            base = at + (MARGIN - 1) + shift
            total = taps[0] * padded[:, pl.ds(base, slab), :]
            for k in range(1, 4):
                total = total + taps[k] * padded[:, pl.ds(base + k, slab), :]
            total = total.astype(BF16)
            sent[a, 0, pl.ds(at, slab), :] = total[0]
            sent[a, 1, pl.ds(at, slab), :] = total[blocks - 1]
            lev[lax.rem(a, AHEAD + 1), pl.ds(1, blocks), pl.ds(at, slab), :] = total.astype(F32)
            return carry

        lax.fori_loop(0, slabs, mix, 0)

    def align(a):
        shift = doff[1, me * angles + a]
        taps = cubic_taps(dfrac[1, me * angles + a])
        slot = lax.rem(a, AHEAD + 1)
        lane = lax.broadcasted_iota(jnp.int32, (1, slab, LANES), 2)

        def mix(j, carry):
            at = pl.multiple_of(j * slab, slab)
            total = None
            for k in range(4):
                moved = shift + (k - 1)
                back = jnp.where(moved < 0, 1, 0)
                turn = moved + back * LANES
                block = lev[slot, pl.ds(1 - back, blocks + 1), pl.ds(at, slab), :]
                rolled = pltpu.roll(block, lax.rem(LANES - turn, LANES), 2)
                piece = taps[k] * jnp.where(lane < LANES - turn, rolled[0:blocks], rolled[1 : blocks + 1])
                total = piece if total is None else total + piece
            out = total.astype(BF16)
            for b in range(blocks):
                al[a, j, :, pl.ds(b * LANES, LANES)] = out[b]
            return carry

        lax.fori_loop(0, slabs, mix, 0)

    def send(a):
        for step in PARTNERS:
            j = partner(step)
            pltpu.make_async_remote_copy(
                al.at[a, j], sino.at[me, a], s_sem.at[a], r_sem.at[a],
                device_id={"ang": j}, device_id_type=MESH,
            ).start()
        pltpu.make_async_copy(al.at[a, me], sino.at[me, a], own_sem.at[a]).start()

    def level_and_send(a):
        level(a)
        for copy in edge_copies(a):
            copy.start()

    def finish(a):
        for copy in edge_copies(a):
            copy.wait_recv()
        slot = lax.rem(a, AHEAD + 1)
        lev[slot, 0] = jnp.where(col > 0, got[a, 0].astype(F32), 0.0)
        lev[slot, blocks + 1] = jnp.where(col < n_col - 1, got[a, 1].astype(F32), 0.0)
        align(a)
        send(a)

    for copy in drift_copies:
        copy.wait()
    offset_copy.wait()
    level(0)
    pl.semaphore_wait(barrier, len(PARTNERS) + 2)
    for copy in edge_copies(0):
        copy.start()
    for a in range(1, AHEAD):
        level_and_send(a)

    def both(a, carry):
        finish(a)
        level_and_send(a + AHEAD)
        return carry

    lax.fori_loop(0, angles - AHEAD, both, 0)

    def last(a, carry):
        finish(a)
        return carry

    lax.fori_loop(angles - AHEAD, angles, last, 0)

    for k in range(3):
        ramp[k] = ramp_tile(RW * (k - 1)).astype(BF16)

    def halo_copies(k):
        return (
            pltpu.make_async_remote_copy(
                sino.at[:, k, :, pl.ds(width - RW, RW)], halo_l.at[:, k], hs_sem.at[0], hr_sem.at[0],
                device_id={"col": right}, device_id_type=MESH,
            ),
            pltpu.make_async_remote_copy(
                sino.at[:, k, :, pl.ds(0, RW)], halo_r.at[:, k], hs_sem.at[1], hr_sem.at[1],
                device_id={"col": left}, device_id_type=MESH,
            ),
        )

    def arrived(k):
        return pltpu.make_async_remote_copy(
            al.at[k, pl.ds(0, slabs - 1)], sino.at[pl.ds(0, slabs - 1), k], s_sem.at[k], r_sem.at[k],
            device_id={"ang": me}, device_id_type=MESH,
        )

    def collect(k, total):
        pltpu.make_async_copy(al.at[k, me], sino.at[me, k], own_sem.at[k]).wait()
        arrived(k).wait_recv()
        for copy in halo_copies(k):
            copy.start()
        return lax.fori_loop(0, slabs, lambda i, t: t + sino[i, k].astype(F32), total)

    total = lax.fori_loop(0, angles, collect, jnp.zeros((slab, width), F32))
    mean[:, pl.ds(MEDGE, width)] = total / float(slabs * angles)

    mean_copies = (
        pltpu.make_async_remote_copy(
            mean.at[:, pl.ds(width, MEDGE)], mean.at[:, pl.ds(0, MEDGE)], ms_sem.at[0], mr_sem.at[0],
            device_id={"col": right}, device_id_type=MESH,
        ),
        pltpu.make_async_remote_copy(
            mean.at[:, pl.ds(MEDGE, MEDGE)], mean.at[:, pl.ds(MEDGE + width, MEDGE)], ms_sem.at[1], mr_sem.at[1],
            device_id={"col": left}, device_id_type=MESH,
        ),
    )
    for copy in mean_copies:
        copy.start()

    def drain(k, carry):
        arrived(k).wait_send()
        for copy in edge_copies(k):
            copy.wait_send()
        return carry

    lax.fori_loop(0, angles, drain, 0)
    for side, halo in ((0, halo_l), (1, halo_r)):
        whole = pltpu.make_async_remote_copy(
            halo, halo, hs_sem.at[side], hr_sem.at[side], device_id={"col": left}, device_id_type=MESH
        )
        whole.wait_send()
        whole.wait_recv()
    for copy in mean_copies:
        copy.wait_send()
        copy.wait_recv()


def filter_kernel(
    sino, halo_l, halo_r, mean, ramp, widths,
    out,
    ends, cyc, kept, obuf, o_sem,
):
    col = lax.axis_index("col")
    n_col = lax.axis_size("col")
    slabs, angles, slab, width = sino.shape
    total_cols = n_col * width
    parts = width // RW

    ends[0] = jnp.where(col > 0, ramp[0], jnp.zeros((RW, RW), BF16))
    ends[1] = jnp.where(col < n_col - 1, ramp[2], jnp.zeros((RW, RW), BF16))

    span = width + 2 * MEDGE
    at = lax.broadcasted_iota(jnp.int32, (slab, span), 1) + (col * width - MEDGE)
    inside = (at >= 0) & (at < total_cols)
    line = lax.broadcasted_iota(jnp.int32, (slab, 1), 0)
    half = jnp.zeros((slab, 1), jnp.int32)
    for r in range(slab):
        half = jnp.where(line == r, widths[r], half)
    centre = jnp.where(inside, mean[...], 0.0)
    running = centre
    for j in range(1, BWMAX + 1):
        pair = pltpu.roll(centre, j, 1) + pltpu.roll(centre, span - j, 1)
        running = running + jnp.where(half >= j, pair, 0.0)
    count = jnp.minimum(at, half) + jnp.minimum(total_cols - 1 - at, half) + 1
    count = jnp.maximum(count, 1).astype(F32)
    cycle = jnp.where(inside, centre - running / count, 0.0)
    first = cycle.astype(BF16)
    rest = cycle - first.astype(F32)
    second = rest.astype(BF16)
    third = (rest - second.astype(F32)).astype(BF16)
    cyc[0:slab] = first
    cyc[slab : 2 * slab] = second
    cyc[2 * slab : 3 * slab] = third
    for n in range(parts):
        acc = jnp.zeros((3 * slab, RW), F32)
        for k in range(3):
            acc = acc + jnp.dot(
                cyc[:, pl.ds(MEDGE + RW * (n + k - 1), RW)], ramp[k], preferred_element_type=F32
            )
        kept[:, pl.ds(n * RW, RW)] = acc[0:slab] + acc[slab : 2 * slab] + acc[2 * slab : 3 * slab]

    group = obuf.shape[1]
    steps = slabs // group

    def put(g):
        slot = lax.rem(g, 2)
        return pltpu.make_async_copy(obuf.at[slot], out.at[pl.ds(g * group, group)], o_sem.at[slot])

    lines = group * angles * slab

    def filt(g, carry):
        slot = lax.rem(g, 2)

        @pl.when(g >= 2)
        def _():
            put(g - 2).wait()

        def window(m):
            if m < 0:
                return halo_l[pl.ds(g * group, group)].reshape(lines, RW)
            if m == parts:
                return halo_r[pl.ds(g * group, group)].reshape(lines, RW)
            return sino[pl.ds(g * group, group), :, :, pl.ds(m * RW, RW)].reshape(lines, RW)

        for n in range(parts):
            acc = jnp.dot(window(n), ramp[1], preferred_element_type=F32)
            acc = acc + jnp.dot(window(n - 1), ends[0] if n == 0 else ramp[0], preferred_element_type=F32)
            acc = acc + jnp.dot(
                window(n + 1), ends[1] if n == parts - 1 else ramp[2], preferred_element_type=F32
            )
            lanes = pl.ds(n * RW, RW)
            obuf[slot, :, :, :, lanes] = acc.reshape(group, angles, slab, RW) - kept[:, lanes]
        put(g).start()
        return carry

    lax.fori_loop(0, steps, filt, 0)
    put(steps - 2).wait()
    put(steps - 1).wait()


def on_device(projections, detector_offset, drift_offsets, drift_fractions, cycle_widths):
    angles, rows, width = projections.shape
    slab = cycle_widths.shape[0]
    slabs = rows // slab
    blocks = width // LANES
    vmem = pl.BlockSpec(memory_space=pltpu.VMEM)
    smem = pl.BlockSpec(memory_space=pltpu.SMEM)
    hbm = pl.BlockSpec(memory_space=pltpu.HBM)
    dma = pltpu.SemaphoreType.DMA
    held = pl.pallas_call(
        exchange_kernel,
        name="exchange",
        out_shape=(
            pltpu.VMEM((slabs, angles, slab, width), BF16),
            pltpu.VMEM((slabs, angles, slab, RW), BF16),
            pltpu.VMEM((slabs, angles, slab, RW), BF16),
            pltpu.VMEM((slab, width + 2 * MEDGE), F32),
            pltpu.VMEM((3, RW, RW), BF16),
        ),
        in_specs=[hbm] * 4,
        out_specs=(vmem,) * 5,
        scratch_shapes=[
            pltpu.VMEM((angles, rows, width), BF16),
            pltpu.VMEM((rows, width), F32),
            pltpu.SMEM(drift_offsets.shape, jnp.int32),
            pltpu.SMEM(drift_offsets.shape, jnp.int32),
            pltpu.VMEM((blocks, rows + 2 * MARGIN, LANES), F32),
            pltpu.VMEM((AHEAD + 1, blocks + 2, rows, LANES), F32),
            pltpu.VMEM((angles, 2, rows, LANES), BF16),
            pltpu.VMEM((angles, 2, rows, LANES), BF16),
            pltpu.VMEM((angles, slabs, slab, width), BF16),
            dma((2,)),
            dma((angles,)),
            dma,
            dma((angles, 2)),
            dma((angles, 2)),
            dma((angles,)),
            dma((angles,)),
            dma((angles,)),
            dma((2,)),
            dma((2,)),
            dma((2,)),
            dma((2,)),
        ],
        compiler_params=pltpu.CompilerParams(
            collective_id=0, has_side_effects=True, vmem_limit_bytes=44 * 1024 * 1024
        ),
        cost_estimate=pl.CostEstimate(flops=40_000_000, bytes_accessed=6 * 1024 * 1024, transcendentals=0),
    )(projections, detector_offset, drift_offsets, drift_fractions)
    group = 2
    filtered = pl.pallas_call(
        filter_kernel,
        name="filter",
        out_shape=jax.ShapeDtypeStruct((slabs, angles, slab, width), F32),
        in_specs=[vmem] * 5 + [smem],
        out_specs=hbm,
        scratch_shapes=[
            pltpu.VMEM((2, RW, RW), BF16),
            pltpu.VMEM((3 * slab, width + 2 * MEDGE), BF16),
            pltpu.VMEM((slab, width), F32),
            pltpu.VMEM((2, group, angles, slab, width), F32),
            dma((2,)),
        ],
        compiler_params=pltpu.CompilerParams(vmem_limit_bytes=24 * 1024 * 1024),
        cost_estimate=pl.CostEstimate(flops=3_300_000_000, bytes_accessed=8 * 1024 * 1024, transcendentals=0),
    )(*held, cycle_widths)
    return filtered.reshape(slabs * angles, slab, width)


def solution(mesh):
    placed = (P("ang", None, "col"), P(None, "col"), P(), P(), P("ang"))
    return jax.shard_map(
        on_device, mesh=mesh, in_specs=placed, out_specs=P(None, "ang", "col"), check_vma=False
    )
```

```python
import functools
import math

import jax
import jax.numpy as jnp
from jax import lax
from jax.experimental import pallas as pl
from jax.experimental.pallas import tpu as pltpu
from jax.sharding import PartitionSpec as P

BWMAX = 16
RW = 256
MESH = pl.DeviceIdType.MESH
F32 = jnp.float32
BF16 = jnp.bfloat16

STRIDE = 7
SIDE = 4
MARGIN = 8
LANES = 128
AHEAD = 2
MEDGE = 384


def cubic_taps(fraction):
    t = fraction.astype(F32) / 256.0
    t2 = t * t
    t3 = t2 * t
    return (
        (-t3 + 2.0 * t2 - t) * 0.5,
        (3.0 * t3 - 5.0 * t2 + 2.0) * 0.5,
        (-3.0 * t3 + 4.0 * t2 + t) * 0.5,
        (t3 - t2) * 0.5,
    )


def ramp_tile(shift):
    rows = lax.broadcasted_iota(jnp.int32, (RW, RW), 0)
    cols = lax.broadcasted_iota(jnp.int32, (RW, RW), 1)
    n = rows - cols + shift
    odd = (n & 1) == 1
    safe = jnp.where(n == 0, 1, n).astype(F32)
    value = jnp.where(n == 0, 0.25, jnp.where(odd, -1.0 / (math.pi**2 * safe * safe), 0.0))
    return jnp.where(jnp.abs(n) <= RW, value, 0.0)


def exchange_kernel(
    proj, offset, doff_in, dfrac_in, widths_in,
    part, kept,
    pbuf, obuf, doff, dfrac, widths, padded, lev, sent, got, al, sino, halo_l, halo_r, mean, cyc, ramp, ends,
    d_sem, p_sem, o_sem, es_sem, er_sem, own_sem, s_sem, r_sem, hs_sem, hr_sem, ms_sem, mr_sem,
):
    me = lax.axis_index("ang")
    col = lax.axis_index("col")
    n_col = lax.axis_size("col")
    angles, rows, width = proj.shape
    slabs, _, slab, _ = sino.shape
    blocks = width // LANES
    y, x = me // SIDE, lax.rem(me, SIDE)
    sign = 1 - 2 * lax.rem(col, 2)
    left = lax.rem(col + n_col - 1, n_col)
    right = lax.rem(col + 1, n_col)

    def partner(n):
        place = lax.rem(STRIDE * n, slabs)
        return lax.rem(y + SIDE + sign * (place // SIDE), SIDE) * SIDE + lax.rem(
            x + SIDE + sign * lax.rem(place, SIDE), SIDE
        )

    def frame_copy(a):
        return pltpu.make_async_copy(proj.at[a], pbuf.at[a], p_sem.at[a])

    drift_copies = (
        pltpu.make_async_copy(doff_in, doff, d_sem.at[0]),
        pltpu.make_async_copy(dfrac_in, dfrac, d_sem.at[1]),
        pltpu.make_async_copy(widths_in, widths, d_sem.at[2]),
    )
    for copy in drift_copies:
        copy.start()
    offset_copy = pltpu.make_async_copy(offset, obuf, o_sem)
    frame_copy(0).start()
    offset_copy.start()
    for a in range(1, angles):
        frame_copy(a).start()

    barrier = pltpu.get_barrier_semaphore()
    for n in range(1, slabs):
        pl.semaphore_signal(barrier, 1, device_id={"ang": partner(n)}, device_id_type=MESH)
    for neighbour in (left, right):
        pl.semaphore_signal(barrier, 1, device_id={"col": neighbour}, device_id_type=MESH)

    zeros = jnp.zeros((blocks, MARGIN, LANES), F32)
    padded[:, 0:MARGIN, :] = zeros
    padded[:, MARGIN + rows : 2 * MARGIN + rows, :] = zeros

    def edge_copies(a):
        return (
            pltpu.make_async_remote_copy(
                sent.at[a, 1], got.at[a, 0], es_sem.at[a, 0], er_sem.at[a, 0],
                device_id={"col": right}, device_id_type=MESH,
            ),
            pltpu.make_async_remote_copy(
                sent.at[a, 0], got.at[a, 1], es_sem.at[a, 1], er_sem.at[a, 1],
                device_id={"col": left}, device_id_type=MESH,
            ),
        )

    def level(a):
        frame_copy(a).wait()
        shift = doff[0, me * angles + a]
        taps = cubic_taps(dfrac[0, me * angles + a])

        def fill(j, carry):
            at = pl.multiple_of(j * slab, slab)
            for b in range(blocks):
                lanes = pl.ds(b * LANES, LANES)
                padded[b, pl.ds(at + MARGIN, slab), :] = (
                    pbuf[a, pl.ds(at, slab), lanes].astype(F32) + obuf[pl.ds(at, slab), lanes]
                )
            return carry

        lax.fori_loop(0, slabs, fill, 0)

        def mix(j, carry):
            at = pl.multiple_of(j * slab, slab)
            base = at + (MARGIN - 1) + shift
            total = taps[0] * padded[:, pl.ds(base, slab), :]
            for k in range(1, 4):
                total = total + taps[k] * padded[:, pl.ds(base + k, slab), :]
            total = total.astype(BF16)
            sent[a, 0, pl.ds(at, slab), :] = total[0]
            sent[a, 1, pl.ds(at, slab), :] = total[blocks - 1]
            lev[lax.rem(a, AHEAD + 1), pl.ds(1, blocks), pl.ds(at, slab), :] = total.astype(F32)
            return carry

        lax.fori_loop(0, slabs, mix, 0)

    def align_and_send(a):
        shift = doff[1, me * angles + a]
        taps = cubic_taps(dfrac[1, me * angles + a])
        slot = lax.rem(a, AHEAD + 1)
        lane = lax.broadcasted_iota(jnp.int32, (1, slab, LANES), 2)

        def mix(n, carry):
            j = partner(n)
            at = pl.multiple_of(j * slab, slab)
            total = None
            for k in range(4):
                moved = shift + (k - 1)
                back = jnp.where(moved < 0, 1, 0)
                turn = moved + back * LANES
                block = lev[slot, pl.ds(1 - back, blocks + 1), pl.ds(at, slab), :]
                rolled = pltpu.roll(block, lax.rem(LANES - turn, LANES), 2)
                piece = taps[k] * jnp.where(lane < LANES - turn, rolled[0:blocks], rolled[1 : blocks + 1])
                total = piece if total is None else total + piece
            out = total.astype(BF16)
            for b in range(blocks):
                al[a, j, :, pl.ds(b * LANES, LANES)] = out[b]

            @pl.when(n > 1)
            def _():
                to = partner(n - 1)
                pltpu.make_async_remote_copy(
                    al.at[a, to], sino.at[me, a], s_sem.at[a], r_sem.at[a],
                    device_id={"ang": to}, device_id_type=MESH,
                ).start()

            return carry

        lax.fori_loop(1, slabs + 1, mix, 0)
        pltpu.make_async_copy(al.at[a, me], sino.at[me, a], own_sem.at[a]).start()

    def level_and_send(a):
        level(a)
        for copy in edge_copies(a):
            copy.start()

    def finish(a):
        for copy in edge_copies(a):
            copy.wait_recv()
        slot = lax.rem(a, AHEAD + 1)
        lev[slot, 0] = jnp.where(col > 0, got[a, 0].astype(F32), 0.0)
        lev[slot, blocks + 1] = jnp.where(col < n_col - 1, got[a, 1].astype(F32), 0.0)
        align_and_send(a)

    for copy in drift_copies:
        copy.wait()
    offset_copy.wait()
    level(0)
    pl.semaphore_wait(barrier, slabs + 1)
    for copy in edge_copies(0):
        copy.start()
    for a in range(1, AHEAD):
        level_and_send(a)

    def both(a, carry):
        finish(a)
        level_and_send(a + AHEAD)
        return carry

    lax.fori_loop(0, angles - AHEAD, both, 0)

    def last(a, carry):
        finish(a)
        return carry

    lax.fori_loop(angles - AHEAD, angles, last, 0)

    for k in range(3):
        ramp[k] = ramp_tile(RW * (k - 1)).astype(BF16)

    ends[0] = jnp.where(col > 0, ramp[0], jnp.zeros((RW, RW), BF16))
    ends[1] = jnp.where(col < n_col - 1, ramp[2], jnp.zeros((RW, RW), BF16))

    def halo_copies(k):
        return (
            pltpu.make_async_remote_copy(
                sino.at[:, k, :, pl.ds(width - RW, RW)], halo_l.at[:, k], hs_sem.at[0], hr_sem.at[0, k],
                device_id={"col": right}, device_id_type=MESH,
            ),
            pltpu.make_async_remote_copy(
                sino.at[:, k, :, pl.ds(0, RW)], halo_r.at[:, k], hs_sem.at[1], hr_sem.at[1, k],
                device_id={"col": left}, device_id_type=MESH,
            ),
        )

    def arrived(k):
        return pltpu.make_async_remote_copy(
            al.at[k, pl.ds(0, slabs - 1)], sino.at[pl.ds(0, slabs - 1), k], s_sem.at[k], r_sem.at[k],
            device_id={"ang": me}, device_id_type=MESH,
        )

    def collect(k, total):
        pltpu.make_async_copy(al.at[k, me], sino.at[me, k], own_sem.at[k]).wait()
        arrived(k).wait_recv()
        return lax.fori_loop(0, slabs, lambda i, t: t + sino[i, k].astype(F32), total)

    def pass_on(k):
        for copy in halo_copies(k):
            copy.start()

    parts = width // RW

    def filt(k):
        for copy in halo_copies(k):
            copy.wait_recv()

        def window(m):
            if m < 0:
                return halo_l[:, k].reshape(rows, RW)
            if m == parts:
                return halo_r[:, k].reshape(rows, RW)
            return sino[:, k, :, pl.ds(m * RW, RW)].reshape(rows, RW)

        for n in range(parts):
            acc = jnp.dot(window(n), ramp[1], preferred_element_type=F32)
            acc = acc + jnp.dot(window(n - 1), ends[0] if n == 0 else ramp[0], preferred_element_type=F32)
            acc = acc + jnp.dot(
                window(n + 1), ends[1] if n == parts - 1 else ramp[2], preferred_element_type=F32
            )
            part[:, k, :, pl.ds(n * RW, RW)] = acc.reshape(slabs, slab, RW)

    total = collect(0, jnp.zeros((slab, width), F32))
    pass_on(0)

    def middle(k, total):
        total = collect(k, total)
        pass_on(k)
        filt(k - 1)
        return total

    total = lax.fori_loop(1, angles - 1, middle, total)
    total = collect(angles - 1, total)
    mean[:, pl.ds(MEDGE, width)] = total / float(slabs * angles)

    mean_copies = (
        pltpu.make_async_remote_copy(
            mean.at[:, pl.ds(width, MEDGE)], mean.at[:, pl.ds(0, MEDGE)], ms_sem.at[0], mr_sem.at[0],
            device_id={"col": right}, device_id_type=MESH,
        ),
        pltpu.make_async_remote_copy(
            mean.at[:, pl.ds(MEDGE, MEDGE)], mean.at[:, pl.ds(MEDGE + width, MEDGE)], ms_sem.at[1], mr_sem.at[1],
            device_id={"col": left}, device_id_type=MESH,
        ),
    )
    for copy in mean_copies:
        copy.start()
    pass_on(angles - 1)
    filt(angles - 2)

    def drain(k, carry):
        arrived(k).wait_send()
        for copy in edge_copies(k):
            copy.wait_send()
        return carry

    lax.fori_loop(0, angles, drain, 0)
    for copy in mean_copies:
        copy.wait_recv()

    total_cols = n_col * width
    span = width + 2 * MEDGE
    at = lax.broadcasted_iota(jnp.int32, (slab, span), 1) + (col * width - MEDGE)
    inside = (at >= 0) & (at < total_cols)
    line = lax.broadcasted_iota(jnp.int32, (slab, 1), 0)
    half = jnp.zeros((slab, 1), jnp.int32)
    for r in range(slab):
        half = jnp.where(line == r, widths[r], half)
    centre = jnp.where(inside, mean[...], 0.0)
    running = centre
    for j in range(1, BWMAX + 1):
        pair = pltpu.roll(centre, j, 1) + pltpu.roll(centre, span - j, 1)
        running = running + jnp.where(half >= j, pair, 0.0)
    count = jnp.minimum(at, half) + jnp.minimum(total_cols - 1 - at, half) + 1
    count = jnp.maximum(count, 1).astype(F32)
    cycle = jnp.where(inside, centre - running / count, 0.0)
    first = cycle.astype(BF16)
    rest = cycle - first.astype(F32)
    second = rest.astype(BF16)
    third = (rest - second.astype(F32)).astype(BF16)
    cyc[0:slab] = first
    cyc[slab : 2 * slab] = second
    cyc[2 * slab : 3 * slab] = third
    for n in range(parts):
        acc = jnp.zeros((3 * slab, RW), F32)
        for k in range(3):
            acc = acc + jnp.dot(
                cyc[:, pl.ds(MEDGE + RW * (n + k - 1), RW)], ramp[k], preferred_element_type=F32
            )
        kept[:, pl.ds(n * RW, RW)] = acc[0:slab] + acc[slab : 2 * slab] + acc[2 * slab : 3 * slab]

    filt(angles - 1)
    for side, halo in ((0, halo_l), (1, halo_r)):
        pltpu.make_async_remote_copy(
            halo, halo, hs_sem.at[side], hr_sem.at[side, 0], device_id={"col": left}, device_id_type=MESH
        ).wait_send()
    for copy in mean_copies:
        copy.wait_send()


def subtract_kernel(part, kept, out, obuf, o_sem):
    slabs = part.shape[0]

    def put(i):
        return pltpu.make_async_copy(obuf.at[i], out.at[i], o_sem.at[i])

    def step(i, carry):
        obuf[i] = part[i] - kept[...]
        put(i).start()
        return carry

    def wait(i, carry):
        put(i).wait()
        return carry

    lax.fori_loop(0, slabs, step, 0)
    lax.fori_loop(0, slabs, wait, 0)


def on_device(projections, detector_offset, drift_offsets, drift_fractions, cycle_widths):
    angles, rows, width = projections.shape
    slab = cycle_widths.shape[0]
    slabs = rows // slab
    blocks = width // LANES
    vmem = pl.BlockSpec(memory_space=pltpu.VMEM)
    hbm = pl.BlockSpec(memory_space=pltpu.HBM)
    dma = pltpu.SemaphoreType.DMA
    given = (projections, detector_offset, drift_offsets, drift_fractions, cycle_widths)
    part, kept = pl.pallas_call(
        exchange_kernel,
        name="exchange",
        out_shape=(
            pltpu.VMEM((slabs, angles, slab, width), F32),
            pltpu.VMEM((slab, width), F32),
        ),
        in_specs=[hbm] * 5,
        out_specs=(vmem,) * 2,
        scratch_shapes=[
            pltpu.VMEM((angles, rows, width), BF16),
            pltpu.VMEM((rows, width), F32),
            pltpu.SMEM(drift_offsets.shape, jnp.int32),
            pltpu.SMEM(drift_offsets.shape, jnp.int32),
            pltpu.SMEM(cycle_widths.shape, jnp.int32),
            pltpu.VMEM((blocks, rows + 2 * MARGIN, LANES), F32),
            pltpu.VMEM((AHEAD + 1, blocks + 2, rows, LANES), F32),
            pltpu.VMEM((angles, 2, rows, LANES), BF16),
            pltpu.VMEM((angles, 2, rows, LANES), BF16),
            pltpu.VMEM((angles, slabs, slab, width), BF16),
            pltpu.VMEM((slabs, angles, slab, width), BF16),
            pltpu.VMEM((slabs, angles, slab, RW), BF16),
            pltpu.VMEM((slabs, angles, slab, RW), BF16),
            pltpu.VMEM((slab, width + 2 * MEDGE), F32),
            pltpu.VMEM((3 * slab, width + 2 * MEDGE), BF16),
            pltpu.VMEM((3, RW, RW), BF16),
            pltpu.VMEM((2, RW, RW), BF16),
            dma((3,)),
            dma((angles,)),
            dma,
            dma((angles, 2)),
            dma((angles, 2)),
            dma((angles,)),
            dma((angles,)),
            dma((angles,)),
            dma((2,)),
            dma((2, angles)),
            dma((2,)),
            dma((2,)),
        ],
        compiler_params=pltpu.CompilerParams(
            collective_id=0, has_side_effects=True, vmem_limit_bytes=54 * 1024 * 1024
        ),
    )(*(pltpu.with_memory_space_constraint(a, pltpu.HBM) for a in given))
    filtered = pl.pallas_call(
        subtract_kernel,
        name="subtract",
        out_shape=jax.ShapeDtypeStruct((slabs, angles, slab, width), F32),
        in_specs=[vmem] * 2,
        out_specs=hbm,
        scratch_shapes=[pltpu.VMEM((slabs, angles, slab, width), F32), dma((slabs,))],
        compiler_params=pltpu.CompilerParams(vmem_limit_bytes=24 * 1024 * 1024),
    )(part, kept)
    return filtered.reshape(slabs * angles, slab, width)


def solution(mesh):
    placed = (P("ang", None, "col"), P(None, "col"), P(), P(), P("ang"))
    return jax.shard_map(
        on_device, mesh=mesh, in_specs=placed, out_specs=P(None, "ang", "col"), check_vma=False
    )
```

```python
import functools
import math

import jax
import jax.numpy as jnp
from jax import lax
from jax.experimental import pallas as pl
from jax.experimental.pallas import tpu as pltpu
from jax.sharding import PartitionSpec as P

BWMAX = 16
RW = 256
MESH = pl.DeviceIdType.MESH
F32 = jnp.float32
BF16 = jnp.bfloat16

ORDER = (10, 6, 11, 14, 9, 2, 8, 5, 15, 7, 13, 1, 4, 3, 12, 0)
DIGITS = 7
SIDE = 4
MARGIN = 8
LANES = 128
AHEAD = 2
MEDGE = 384


def cubic_taps(fraction):
    t = fraction.astype(F32) / 256.0
    t2 = t * t
    t3 = t2 * t
    return (
        (-t3 + 2.0 * t2 - t) * 0.5,
        (3.0 * t3 - 5.0 * t2 + 2.0) * 0.5,
        (-3.0 * t3 + 4.0 * t2 + t) * 0.5,
        (t3 - t2) * 0.5,
    )


def ramp_tile(shift):
    rows = lax.broadcasted_iota(jnp.int32, (RW, RW), 0)
    cols = lax.broadcasted_iota(jnp.int32, (RW, RW), 1)
    n = rows - cols + shift
    odd = (n & 1) == 1
    safe = jnp.where(n == 0, 1, n).astype(F32)
    value = jnp.where(n == 0, 0.25, jnp.where(odd, -1.0 / (math.pi**2 * safe * safe), 0.0))
    return jnp.where(jnp.abs(n) <= RW, value, 0.0)


def exchange_kernel(
    proj, offset, doff_in, dfrac_in, widths_in,
    part, kept,
    pbuf, obuf, doff, dfrac, widths, padded, lev, sent, got, al, al_outer, sino, halo_l, halo_r, mean, cyc, ramp, ends,
    d_sem, p_sem, o_sem, es_sem, er_sem, own_sem, s_sem, r_sem, hs_sem, hr_sem, ms_sem, mr_sem,
):
    me = lax.axis_index("ang")
    col = lax.axis_index("col")
    n_col = lax.axis_size("col")
    angles, rows, width = proj.shape
    slabs, _, slab, _ = sino.shape
    blocks = width // LANES
    y, x = me // SIDE, lax.rem(me, SIDE)
    sign = 1 - 2 * lax.rem(col, 2)
    left = lax.rem(col + n_col - 1, n_col)
    right = lax.rem(col + 1, n_col)

    def partner(n):
        if isinstance(n, int):
            place = ORDER[n]
        else:
            place = 0
            for first in range(0, slabs, DIGITS):
                code = sum(p << (4 * d) for d, p in enumerate(ORDER[first : first + DIGITS]))
                here = jnp.clip(n - first, 0, DIGITS - 1)
                digit = lax.shift_right_logical(jnp.int32(code), 4 * here) & 15
                place = jnp.where(n >= first, digit, place)
        return lax.rem(y + SIDE + sign * (place // SIDE), SIDE) * SIDE + lax.rem(
            x + SIDE + sign * lax.rem(place, SIDE), SIDE
        )

    def frame_copy(a):
        return pltpu.make_async_copy(proj.at[a], pbuf.at[a], p_sem.at[a])

    drift_copies = (
        pltpu.make_async_copy(doff_in, doff, d_sem.at[0]),
        pltpu.make_async_copy(dfrac_in, dfrac, d_sem.at[1]),
        pltpu.make_async_copy(widths_in, widths, d_sem.at[2]),
    )
    for copy in drift_copies:
        copy.start()
    offset_copy = pltpu.make_async_copy(offset, obuf, o_sem)
    frame_copy(0).start()
    offset_copy.start()
    for a in range(1, angles):
        frame_copy(a).start()

    barrier = pltpu.get_barrier_semaphore()
    for n in range(slabs - 1):
        pl.semaphore_signal(barrier, 1, device_id={"ang": partner(n)}, device_id_type=MESH)
    for neighbour in (left, right):
        pl.semaphore_signal(barrier, 1, device_id={"col": neighbour}, device_id_type=MESH)

    zeros = jnp.zeros((blocks, MARGIN, LANES), F32)
    padded[:, 0:MARGIN, :] = zeros
    padded[:, MARGIN + rows : 2 * MARGIN + rows, :] = zeros

    def edge_copies(a):
        return (
            pltpu.make_async_remote_copy(
                sent.at[a, 1], got.at[a, 0], es_sem.at[a, 0], er_sem.at[a, 0],
                device_id={"col": right}, device_id_type=MESH,
            ),
            pltpu.make_async_remote_copy(
                sent.at[a, 0], got.at[a, 1], es_sem.at[a, 1], er_sem.at[a, 1],
                device_id={"col": left}, device_id_type=MESH,
            ),
        )

    def level(a):
        frame_copy(a).wait()
        shift = doff[0, me * angles + a]
        taps = cubic_taps(dfrac[0, me * angles + a])

        def fill(j, carry):
            at = pl.multiple_of(j * slab, slab)
            for b in range(blocks):
                lanes = pl.ds(b * LANES, LANES)
                padded[b, pl.ds(at + MARGIN, slab), :] = (
                    pbuf[a, pl.ds(at, slab), lanes].astype(F32) + obuf[pl.ds(at, slab), lanes]
                )
            return carry

        lax.fori_loop(0, slabs, fill, 0)

        def mix(j, carry):
            at = pl.multiple_of(j * slab, slab)
            base = at + (MARGIN - 1) + shift
            total = taps[0] * padded[:, pl.ds(base, slab), :]
            for k in range(1, 4):
                total = total + taps[k] * padded[:, pl.ds(base + k, slab), :]
            total = total.astype(BF16)
            sent[a, 0, pl.ds(at, slab), :] = total[0]
            sent[a, 1, pl.ds(at, slab), :] = total[blocks - 1]
            lev[lax.rem(a, AHEAD + 1), pl.ds(1, blocks), pl.ds(at, slab), :] = total.astype(F32)
            return carry

        lax.fori_loop(0, slabs, mix, 0)

    def rows_to(to, a, buf, piece, sem):
        lanes = pl.ds(piece[0] * LANES, piece[1] * LANES)
        return pltpu.make_async_remote_copy(
            buf.at[to, :, lanes], sino.at[me, a, :, lanes], s_sem.at[sem], r_sem.at[sem],
            device_id={"ang": to}, device_id_type=MESH,
        )

    def align_and_send(a, buf, sem, made, gone):
        shift = doff[1, me * angles + a]
        taps = cubic_taps(dfrac[1, me * angles + a])
        slot = lax.rem(a, AHEAD + 1)
        lane = lax.broadcasted_iota(jnp.int32, (1, slab, LANES), 2)

        def mix(n, carry):
            j = partner(n)
            at = pl.multiple_of(j * slab, slab)
            for first, number in made:
                total = None
                for k in range(4):
                    moved = shift + (k - 1)
                    back = jnp.where(moved < 0, 1, 0)
                    turn = moved + back * LANES
                    block = lev[slot, pl.ds(first + 1 - back, number + 1), pl.ds(at, slab), :]
                    rolled = pltpu.roll(block, lax.rem(LANES - turn, LANES), 2)
                    piece = taps[k] * jnp.where(lane < LANES - turn, rolled[0:number], rolled[1 : number + 1])
                    total = piece if total is None else total + piece
                out = total.astype(BF16)
                for b in range(number):
                    buf[j, :, pl.ds((first + b) * LANES, LANES)] = out[b]

            @pl.when(n > 0)
            def _():
                for piece in gone:
                    rows_to(partner(n - 1), a, buf, piece, sem).start()

            return carry

        lax.fori_loop(0, slabs, mix, 0)

    def own_copy(a, buf, piece, sem):
        lanes = pl.ds(piece[0] * LANES, piece[1] * LANES)
        return pltpu.make_async_copy(buf.at[me, :, lanes], sino.at[me, a, :, lanes], own_sem.at[sem])

    def level_and_send(a):
        level(a)
        for copy in edge_copies(a):
            copy.start()

    def take_edges(a):
        for copy in edge_copies(a):
            copy.wait_recv()
        slot = lax.rem(a, AHEAD + 1)
        lev[slot, 0] = jnp.where(col > 0, got[a, 0].astype(F32), 0.0)
        lev[slot, blocks + 1] = jnp.where(col < n_col - 1, got[a, 1].astype(F32), 0.0)

    whole = (0, blocks)
    inner = (1, blocks - 2)
    outer = ((0, 1), (blocks - 1, 1))
    rim = MEDGE // LANES
    rims = ((0, rim), (blocks - rim, rim))
    core = (rim, blocks - 2 * rim)
    late = angles - 2
    outer_sem, core_sem = angles, angles + 1

    for copy in drift_copies:
        copy.wait()
    offset_copy.wait()
    level(0)
    pl.semaphore_wait(barrier, slabs + 1)
    for copy in edge_copies(0):
        copy.start()
    align_and_send(0, al.at[0], 0, (inner,), (inner,))
    own_copy(0, al.at[0], inner, 0).start()
    level_and_send(1)
    take_edges(0)
    align_and_send(0, al_outer, outer_sem, outer, outer)
    for n, piece in enumerate(outer):
        own_copy(0, al_outer, piece, angles + n).start()
    for a in range(2, AHEAD + 1):
        level_and_send(a)

    def both(a, carry):
        take_edges(a)
        align_and_send(a, al.at[a], a, (whole,), (whole,))
        own_copy(a, al.at[a], whole, a).start()
        level_and_send(a + AHEAD)
        return carry

    lax.fori_loop(1, angles - AHEAD, both, 0)

    def last(a, carry):
        take_edges(a)
        align_and_send(a, al.at[a], a, (whole,), rims)
        own_copy(a, al.at[a], whole, a).start()
        return carry

    lax.fori_loop(late, angles, last, 0)

    def last_core(a, carry):
        def one(n, carry):
            rows_to(partner(n), a, al.at[a], core, core_sem + (a - late)).start()
            return carry

        return lax.fori_loop(0, slabs - 1, one, carry)

    lax.fori_loop(late, angles, last_core, 0)

    for k in range(3):
        ramp[k] = ramp_tile(RW * (k - 1)).astype(BF16)

    ends[0] = jnp.where(col > 0, ramp[0], jnp.zeros((RW, RW), BF16))
    ends[1] = jnp.where(col < n_col - 1, ramp[2], jnp.zeros((RW, RW), BF16))

    def halo_copies(k):
        return (
            pltpu.make_async_remote_copy(
                sino.at[:, k, :, pl.ds(width - RW, RW)], halo_l.at[:, k], hs_sem.at[0], hr_sem.at[0, k],
                device_id={"col": right}, device_id_type=MESH,
            ),
            pltpu.make_async_remote_copy(
                sino.at[:, k, :, pl.ds(0, RW)], halo_r.at[:, k], hs_sem.at[1], hr_sem.at[1, k],
                device_id={"col": left}, device_id_type=MESH,
            ),
        )

    def arrived(sem, width):
        part_of = sino.at[pl.ds(0, slabs - 1), 0, :, pl.ds(0, width)]
        return pltpu.make_async_remote_copy(
            part_of, part_of, s_sem.at[sem], r_sem.at[sem], device_id={"ang": me}, device_id_type=MESH
        )

    def summed(k, first, number, total):
        lanes = pl.ds(first * LANES, number * LANES)
        return lax.fori_loop(0, slabs, lambda i, t: t + sino[i, k, :, lanes].astype(F32), total)

    def pass_on(k):
        for copy in halo_copies(k):
            copy.start()

    parts = width // RW

    def filt(k):
        for copy in halo_copies(k):
            copy.wait_recv()

        def window(m):
            if m < 0:
                return halo_l[:, k].reshape(rows, RW)
            if m == parts:
                return halo_r[:, k].reshape(rows, RW)
            return sino[:, k, :, pl.ds(m * RW, RW)].reshape(rows, RW)

        for n in range(parts):
            acc = jnp.dot(window(n), ramp[1], preferred_element_type=F32)
            acc = acc + jnp.dot(window(n - 1), ends[0] if n == 0 else ramp[0], preferred_element_type=F32)
            acc = acc + jnp.dot(
                window(n + 1), ends[1] if n == parts - 1 else ramp[2], preferred_element_type=F32
            )
            part[:, k, :, pl.ds(n * RW, RW)] = acc.reshape(slabs, slab, RW)

    own_copy(0, al.at[0], inner, 0).wait()
    for n, piece in enumerate(outer):
        own_copy(0, al_outer, piece, angles + n).wait()
    arrived(0, inner[1] * LANES).wait_recv()
    arrived(outer_sem, 2 * LANES).wait_recv()
    pass_on(0)
    total = summed(0, 0, blocks, jnp.zeros((slab, width), F32))

    def middle(k, total):
        own_copy(k, al.at[k], whole, k).wait()
        arrived(k, width).wait_recv()
        pass_on(k)
        total = summed(k, 0, blocks, total)
        filt(k - 1)
        return total

    total = lax.fori_loop(1, late, middle, total)
    count = float(slabs * angles)
    sides = [total[:, first * LANES : (first + number) * LANES] for first, number in rims]
    centre = total[:, core[0] * LANES : (core[0] + core[1]) * LANES]
    for k in (late, late + 1):
        own_copy(k, al.at[k], whole, k).wait()
        arrived(k, 2 * MEDGE).wait_recv()
        sides = [summed(k, first, number, side) for (first, number), side in zip(rims, sides)]
        if k == late:
            pass_on(k)
    for (first, number), side in zip(rims, sides):
        mean[:, pl.ds(MEDGE + first * LANES, number * LANES)] = side / count

    mean_copies = (
        pltpu.make_async_remote_copy(
            mean.at[:, pl.ds(width, MEDGE)], mean.at[:, pl.ds(0, MEDGE)], ms_sem.at[0], mr_sem.at[0],
            device_id={"col": right}, device_id_type=MESH,
        ),
        pltpu.make_async_remote_copy(
            mean.at[:, pl.ds(MEDGE, MEDGE)], mean.at[:, pl.ds(MEDGE + width, MEDGE)], ms_sem.at[1], mr_sem.at[1],
            device_id={"col": left}, device_id_type=MESH,
        ),
    )
    for copy in mean_copies:
        copy.start()
    pass_on(angles - 1)
    filt(late - 1)

    for a in range(angles):
        arrived(a, inner[1] * LANES if a == 0 else 2 * MEDGE if a >= late else width).wait_send()
        for copy in edge_copies(a):
            copy.wait_send()
    arrived(outer_sem, 2 * LANES).wait_send()

    arrived(core_sem, core[1] * LANES).wait_recv()
    centre = summed(late, core[0], core[1], centre)
    filt(late)
    arrived(core_sem + 1, core[1] * LANES).wait_recv()
    centre = summed(late + 1, core[0], core[1], centre)
    mean[:, pl.ds(MEDGE + core[0] * LANES, core[1] * LANES)] = centre / count
    for copy in mean_copies:
        copy.wait_recv()

    total_cols = n_col * width
    span = width + 2 * MEDGE
    at = lax.broadcasted_iota(jnp.int32, (slab, span), 1) + (col * width - MEDGE)
    inside = (at >= 0) & (at < total_cols)
    line = lax.broadcasted_iota(jnp.int32, (slab, 1), 0)
    half = jnp.zeros((slab, 1), jnp.int32)
    for r in range(slab):
        half = jnp.where(line == r, widths[r], half)
    centre = jnp.where(inside, mean[...], 0.0)
    running = centre
    for j in range(1, BWMAX + 1):
        pair = pltpu.roll(centre, j, 1) + pltpu.roll(centre, span - j, 1)
        running = running + jnp.where(half >= j, pair, 0.0)
    count = jnp.minimum(at, half) + jnp.minimum(total_cols - 1 - at, half) + 1
    count = jnp.maximum(count, 1).astype(F32)
    cycle = jnp.where(inside, centre - running / count, 0.0)
    first = cycle.astype(BF16)
    rest = cycle - first.astype(F32)
    second = rest.astype(BF16)
    third = (rest - second.astype(F32)).astype(BF16)
    cyc[0:slab] = first
    cyc[slab : 2 * slab] = second
    cyc[2 * slab : 3 * slab] = third
    for n in range(parts):
        acc = jnp.zeros((3 * slab, RW), F32)
        for k in range(3):
            acc = acc + jnp.dot(
                cyc[:, pl.ds(MEDGE + RW * (n + k - 1), RW)], ramp[k], preferred_element_type=F32
            )
        kept[:, pl.ds(n * RW, RW)] = acc[0:slab] + acc[slab : 2 * slab] + acc[2 * slab : 3 * slab]

    filt(angles - 1)
    for sem in (core_sem, core_sem + 1):
        arrived(sem, core[1] * LANES).wait_send()
    for side, halo in ((0, halo_l), (1, halo_r)):
        pltpu.make_async_remote_copy(
            halo, halo, hs_sem.at[side], hr_sem.at[side, 0], device_id={"col": left}, device_id_type=MESH
        ).wait_send()
    for copy in mean_copies:
        copy.wait_send()


def subtract_kernel(part, kept, out, obuf, o_sem):
    slabs = part.shape[0]

    def put(i):
        return pltpu.make_async_copy(obuf.at[i], out.at[i], o_sem.at[i])

    def step(i, carry):
        obuf[i] = part[i] - kept[...]
        put(i).start()
        return carry

    def wait(i, carry):
        put(i).wait()
        return carry

    lax.fori_loop(0, slabs, step, 0)
    lax.fori_loop(0, slabs, wait, 0)


def on_device(projections, detector_offset, drift_offsets, drift_fractions, cycle_widths):
    angles, rows, width = projections.shape
    slab = cycle_widths.shape[0]
    slabs = rows // slab
    blocks = width // LANES
    vmem = pl.BlockSpec(memory_space=pltpu.VMEM)
    hbm = pl.BlockSpec(memory_space=pltpu.HBM)
    dma = pltpu.SemaphoreType.DMA
    given = (projections, detector_offset, drift_offsets, drift_fractions, cycle_widths)
    part, kept = pl.pallas_call(
        exchange_kernel,
        name="exchange",
        out_shape=(
            pltpu.VMEM((slabs, angles, slab, width), F32),
            pltpu.VMEM((slab, width), F32),
        ),
        in_specs=[hbm] * 5,
        out_specs=(vmem,) * 2,
        scratch_shapes=[
            pltpu.VMEM((angles, rows, width), BF16),
            pltpu.VMEM((rows, width), F32),
            pltpu.SMEM(drift_offsets.shape, jnp.int32),
            pltpu.SMEM(drift_offsets.shape, jnp.int32),
            pltpu.SMEM(cycle_widths.shape, jnp.int32),
            pltpu.VMEM((blocks, rows + 2 * MARGIN, LANES), F32),
            pltpu.VMEM((AHEAD + 1, blocks + 2, rows, LANES), F32),
            pltpu.VMEM((angles, 2, rows, LANES), BF16),
            pltpu.VMEM((angles, 2, rows, LANES), BF16),
            pltpu.VMEM((angles, slabs, slab, width), BF16),
            pltpu.VMEM((slabs, slab, width), BF16),
            pltpu.VMEM((slabs, angles, slab, width), BF16),
            pltpu.VMEM((slabs, angles, slab, RW), BF16),
            pltpu.VMEM((slabs, angles, slab, RW), BF16),
            pltpu.VMEM((slab, width + 2 * MEDGE), F32),
            pltpu.VMEM((3 * slab, width + 2 * MEDGE), BF16),
            pltpu.VMEM((3, RW, RW), BF16),
            pltpu.VMEM((2, RW, RW), BF16),
            dma((3,)),
            dma((angles,)),
            dma,
            dma((angles, 2)),
            dma((angles, 2)),
            dma((angles + 2,)),
            dma((angles + 3,)),
            dma((angles + 3,)),
            dma((2,)),
            dma((2, angles)),
            dma((2,)),
            dma((2,)),
        ],
        compiler_params=pltpu.CompilerParams(
            collective_id=0, has_side_effects=True, vmem_limit_bytes=54 * 1024 * 1024
        ),
    )(*(pltpu.with_memory_space_constraint(a, pltpu.HBM) for a in given))
    filtered = pl.pallas_call(
        subtract_kernel,
        name="subtract",
        out_shape=jax.ShapeDtypeStruct((slabs, angles, slab, width), F32),
        in_specs=[vmem] * 2,
        out_specs=hbm,
        scratch_shapes=[pltpu.VMEM((slabs, angles, slab, width), F32), dma((slabs,))],
        compiler_params=pltpu.CompilerParams(vmem_limit_bytes=24 * 1024 * 1024),
    )(part, kept)
    return filtered.reshape(slabs * angles, slab, width)


def solution(mesh):
    placed = (P("ang", None, "col"), P(None, "col"), P(), P(), P("ang"))
    return jax.shard_map(
        on_device, mesh=mesh, in_specs=placed, out_specs=P(None, "ang", "col"), check_vma=False
    )
```

```python
import functools
import math

import jax
import jax.numpy as jnp
from jax import lax
from jax.experimental import pallas as pl
from jax.experimental.pallas import tpu as pltpu
from jax.sharding import PartitionSpec as P

BWMAX = 16
RW = 256
MESH = pl.DeviceIdType.MESH
F32 = jnp.float32
BF16 = jnp.bfloat16

ORDER = (10, 6, 11, 14, 9, 2, 8, 5, 15, 7, 13, 1, 4, 3, 12)
SIDE = 4
MARGIN = 8
LANES = 128
AHEAD = 2
MEDGE = 384


def cubic_taps(fraction):
    t = fraction.astype(F32) / 256.0
    t2 = t * t
    t3 = t2 * t
    return (
        (-t3 + 2.0 * t2 - t) * 0.5,
        (3.0 * t3 - 5.0 * t2 + 2.0) * 0.5,
        (-3.0 * t3 + 4.0 * t2 + t) * 0.5,
        (t3 - t2) * 0.5,
    )


def ramp_tile(shift):
    rows = lax.broadcasted_iota(jnp.int32, (RW, RW), 0)
    cols = lax.broadcasted_iota(jnp.int32, (RW, RW), 1)
    n = rows - cols + shift
    odd = (n & 1) == 1
    safe = jnp.where(n == 0, 1, n).astype(F32)
    value = jnp.where(n == 0, 0.25, jnp.where(odd, -1.0 / (math.pi**2 * safe * safe), 0.0))
    return jnp.where(jnp.abs(n) <= RW, value, 0.0)


def exchange_kernel(
    proj, offset, doff_in, dfrac_in, widths_in,
    part, kept,
    pbuf, obuf, doff, dfrac, widths, padded, lev, bands, al, al_outer, sino, halo_l, halo_r, mean, cyc, ramp, ends,
    d_sem, p_sem, o_sem, es_sem, er_sem, own_sem, s_sem, r_sem, hs_sem, hr_sem, ms_sem, mr_sem,
):
    me = lax.axis_index("ang")
    col = lax.axis_index("col")
    n_col = lax.axis_size("col")
    angles, rows, width = proj.shape
    slabs, _, slab, _ = sino.shape
    blocks = width // LANES
    y, x = me // SIDE, lax.rem(me, SIDE)
    sign = 1 - 2 * lax.rem(col, 2)
    left = lax.rem(col + n_col - 1, n_col)
    right = lax.rem(col + 1, n_col)

    def partner(place):
        return lax.rem(y + SIDE + sign * (place // SIDE), SIDE) * SIDE + lax.rem(
            x + SIDE + sign * (place % SIDE), SIDE
        )

    partners = [partner(place) for place in ORDER]

    def frame_copy(a):
        return pltpu.make_async_copy(proj.at[a], pbuf.at[a], p_sem.at[a])

    drift_copies = (
        pltpu.make_async_copy(doff_in, doff, d_sem.at[0]),
        pltpu.make_async_copy(dfrac_in, dfrac, d_sem.at[1]),
        pltpu.make_async_copy(widths_in, widths, d_sem.at[2]),
    )
    for copy in drift_copies:
        copy.start()
    offset_copy = pltpu.make_async_copy(offset, obuf, o_sem)
    frame_copy(0).start()
    offset_copy.start()
    for a in range(1, angles):
        frame_copy(a).start()

    barrier = pltpu.get_barrier_semaphore()
    for to in partners:
        pl.semaphore_signal(barrier, 1, device_id={"ang": to}, device_id_type=MESH)
    for neighbour in (left, right):
        pl.semaphore_signal(barrier, 1, device_id={"col": neighbour}, device_id_type=MESH)

    zeros = jnp.zeros((blocks, MARGIN, LANES), F32)
    padded[:, 0:MARGIN, :] = zeros
    padded[:, MARGIN + rows : 2 * MARGIN + rows, :] = zeros

    def edge_copies(a):
        return (
            pltpu.make_async_remote_copy(
                lev.at[a, :, pl.ds(width, LANES)], lev.at[a, :, pl.ds(0, LANES)],
                es_sem.at[a, 0], er_sem.at[a, 0], device_id={"col": right}, device_id_type=MESH,
            ),
            pltpu.make_async_remote_copy(
                lev.at[a, :, pl.ds(LANES, LANES)], lev.at[a, :, pl.ds(LANES + width, LANES)],
                es_sem.at[a, 1], er_sem.at[a, 1], device_id={"col": left}, device_id_type=MESH,
            ),
        )

    def level(a):
        frame_copy(a).wait()
        shift = doff[0, me * angles + a]
        taps = cubic_taps(dfrac[0, me * angles + a])

        def fill(j, carry):
            at = pl.multiple_of(j * slab, slab)
            for b in range(blocks):
                lanes = pl.ds(b * LANES, LANES)
                padded[b, pl.ds(at + MARGIN, slab), :] = (
                    pbuf[a, pl.ds(at, slab), lanes].astype(F32) + obuf[pl.ds(at, slab), lanes]
                )
            return carry

        lax.fori_loop(0, slabs, fill, 0)

        def mix(j, carry):
            at = pl.multiple_of(j * slab, slab)
            base = at + (MARGIN - 1) + shift
            total = taps[0] * padded[:, pl.ds(base, slab), :]
            for k in range(1, 4):
                total = total + taps[k] * padded[:, pl.ds(base + k, slab), :]
            total = total.astype(BF16)
            for b in range(blocks):
                lev[a, pl.ds(at, slab), pl.ds((b + 1) * LANES, LANES)] = total[b]
            return carry

        lax.fori_loop(0, slabs, mix, 0)

    def rows_to(to, a, buf, piece, sem):
        lanes = pl.ds(piece[0] * LANES, piece[1] * LANES)
        return pltpu.make_async_remote_copy(
            buf.at[to, :, lanes], sino.at[me, a, :, lanes], s_sem.at[sem], r_sem.at[sem],
            device_id={"ang": to}, device_id_type=MESH,
        )

    def weights(a):
        shift = doff[1, me * angles + a]
        taps = cubic_taps(dfrac[1, me * angles + a])
        slot = lax.rem(a, 2)
        step = 64

        def build(i, carry):
            at = pl.multiple_of(i * step, step)
            index = lax.broadcasted_iota(jnp.int32, (step, RW), 0) - lax.broadcasted_iota(jnp.int32, (step, RW), 1)
            index = index + (at - LANES - shift + 1)
            value = jnp.zeros((step, RW), F32)
            for k in range(4):
                value = jnp.where(index == k, taps[k], value)
            for p in range(3):
                piece = value.astype(BF16)
                bands[slot, p, pl.ds(at, step), :] = piece
                value = value - piece.astype(F32)
            return carry

        lax.fori_loop(0, 2 * RW // step, build, 0)

    def align(a, buf, made):
        slot = lax.rem(a, 2)
        for n in made:
            window = lev[a, :, pl.ds(n * RW, 2 * RW)]
            total = jnp.dot(window, bands[slot, 2], preferred_element_type=F32)
            total = total + jnp.dot(window, bands[slot, 1], preferred_element_type=F32)
            total = total + jnp.dot(window, bands[slot, 0], preferred_element_type=F32)
            buf[:, :, pl.ds(n * RW, RW)] = total.astype(BF16).reshape(slabs, slab, RW)

    def send(a, buf, sem, gone):
        for to in partners:
            for piece in gone:
                rows_to(to, a, buf, piece, sem).start()

    def own_copy(a, buf, piece, sem):
        lanes = pl.ds(piece[0] * LANES, piece[1] * LANES)
        return pltpu.make_async_copy(buf.at[me, :, lanes], sino.at[me, a, :, lanes], own_sem.at[sem])

    def level_and_send(a):
        level(a)
        for copy in edge_copies(a):
            copy.start()

    def take_edges(a):
        for copy in edge_copies(a):
            copy.wait_recv()
        before, after = pl.ds(0, LANES), pl.ds(LANES + width, LANES)
        lev[a, :, before] = jnp.where(col > 0, lev[a, :, before].astype(F32), 0.0).astype(BF16)
        lev[a, :, after] = jnp.where(col < n_col - 1, lev[a, :, after].astype(F32), 0.0).astype(BF16)

    whole = (0, blocks)
    step = RW // LANES
    inner = (step, blocks - 2 * step)
    outer = ((0, step), (blocks - step, step))
    parts = width // RW
    rim = MEDGE // LANES
    rims = ((0, rim), (blocks - rim, rim))
    core = (rim, blocks - 2 * rim)
    late = angles - 2
    outer_sem, core_sem = angles, angles + 1

    for copy in drift_copies:
        copy.wait()
    weights(0)
    offset_copy.wait()
    level(0)
    pl.semaphore_wait(barrier, slabs + 1)
    for copy in edge_copies(0):
        copy.start()
    align(0, al.at[0], range(1, parts - 1))
    weights(1)
    send(0, al.at[0], 0, (inner,))
    own_copy(0, al.at[0], inner, 0).start()
    level_and_send(1)
    take_edges(0)
    align(0, al_outer, (0, parts - 1))
    level_and_send(2)
    send(0, al_outer, outer_sem, outer)
    for n, piece in enumerate(outer):
        own_copy(0, al_outer, piece, angles + n).start()

    def both(a, carry):
        take_edges(a)
        align(a, al.at[a], range(parts))
        weights(a + 1)
        send(a, al.at[a], a, (whole,))
        own_copy(a, al.at[a], whole, a).start()
        level_and_send(a + AHEAD)
        return carry

    lax.fori_loop(1, angles - AHEAD, both, 0)

    def last(a, carry):
        take_edges(a)
        align(a, al.at[a], range(parts))
        weights(jnp.minimum(a + 1, angles - 1))
        send(a, al.at[a], a, rims)
        own_copy(a, al.at[a], whole, a).start()
        return carry

    lax.fori_loop(late, angles, last, 0)

    def last_core(a, carry):
        send(a, al.at[a], core_sem + (a - late), (core,))
        return carry

    lax.fori_loop(late, angles, last_core, 0)

    for k in range(3):
        ramp[k] = ramp_tile(RW * (k - 1)).astype(BF16)

    ends[0] = jnp.where(col > 0, ramp[0], jnp.zeros((RW, RW), BF16))
    ends[1] = jnp.where(col < n_col - 1, ramp[2], jnp.zeros((RW, RW), BF16))

    def halo_copies(k):
        return (
            pltpu.make_async_remote_copy(
                sino.at[:, k, :, pl.ds(width - RW, RW)], halo_l.at[:, k], hs_sem.at[0], hr_sem.at[0, k],
                device_id={"col": right}, device_id_type=MESH,
            ),
            pltpu.make_async_remote_copy(
                sino.at[:, k, :, pl.ds(0, RW)], halo_r.at[:, k], hs_sem.at[1], hr_sem.at[1, k],
                device_id={"col": left}, device_id_type=MESH,
            ),
        )

    def arrived(sem, width):
        part_of = sino.at[pl.ds(0, slabs - 1), 0, :, pl.ds(0, width)]
        return pltpu.make_async_remote_copy(
            part_of, part_of, s_sem.at[sem], r_sem.at[sem], device_id={"ang": me}, device_id_type=MESH
        )

    def summed(k, first, number, total):
        lanes = pl.ds(first * LANES, number * LANES)
        return lax.fori_loop(0, slabs, lambda i, t: t + sino[i, k, :, lanes].astype(F32), total)

    def pass_on(k):
        for copy in halo_copies(k):
            copy.start()

    def filt(k):
        for copy in halo_copies(k):
            copy.wait_recv()

        def window(m):
            if m < 0:
                return halo_l[:, k].reshape(rows, RW)
            if m == parts:
                return halo_r[:, k].reshape(rows, RW)
            return sino[:, k, :, pl.ds(m * RW, RW)].reshape(rows, RW)

        for n in range(parts):
            acc = jnp.dot(window(n), ramp[1], preferred_element_type=F32)
            acc = acc + jnp.dot(window(n - 1), ends[0] if n == 0 else ramp[0], preferred_element_type=F32)
            acc = acc + jnp.dot(
                window(n + 1), ends[1] if n == parts - 1 else ramp[2], preferred_element_type=F32
            )
            part[:, k, :, pl.ds(n * RW, RW)] = acc.reshape(slabs, slab, RW)

    own_copy(0, al.at[0], inner, 0).wait()
    for n, piece in enumerate(outer):
        own_copy(0, al_outer, piece, angles + n).wait()
    arrived(0, inner[1] * LANES).wait_recv()
    arrived(outer_sem, 2 * RW).wait_recv()
    pass_on(0)
    total = summed(0, 0, blocks, jnp.zeros((slab, width), F32))

    def middle(k, total):
        own_copy(k, al.at[k], whole, k).wait()
        arrived(k, width).wait_recv()
        pass_on(k)
        total = summed(k, 0, blocks, total)
        filt(k - 1)
        return total

    total = lax.fori_loop(1, late, middle, total)
    count = float(slabs * angles)
    sides = [total[:, first * LANES : (first + number) * LANES] for first, number in rims]
    centre = total[:, core[0] * LANES : (core[0] + core[1]) * LANES]
    for k in (late, late + 1):
        own_copy(k, al.at[k], whole, k).wait()
        arrived(k, 2 * MEDGE).wait_recv()
        sides = [summed(k, first, number, side) for (first, number), side in zip(rims, sides)]
        if k == late:
            pass_on(k)
    for (first, number), side in zip(rims, sides):
        mean[:, pl.ds(MEDGE + first * LANES, number * LANES)] = side / count

    mean_copies = (
        pltpu.make_async_remote_copy(
            mean.at[:, pl.ds(width, MEDGE)], mean.at[:, pl.ds(0, MEDGE)], ms_sem.at[0], mr_sem.at[0],
            device_id={"col": right}, device_id_type=MESH,
        ),
        pltpu.make_async_remote_copy(
            mean.at[:, pl.ds(MEDGE, MEDGE)], mean.at[:, pl.ds(MEDGE + width, MEDGE)], ms_sem.at[1], mr_sem.at[1],
            device_id={"col": left}, device_id_type=MESH,
        ),
    )
    for copy in mean_copies:
        copy.start()
    pass_on(angles - 1)
    filt(late - 1)

    for a in range(angles):
        arrived(a, inner[1] * LANES if a == 0 else 2 * MEDGE if a >= late else width).wait_send()
        for copy in edge_copies(a):
            copy.wait_send()
    arrived(outer_sem, 2 * RW).wait_send()

    arrived(core_sem, core[1] * LANES).wait_recv()
    centre = summed(late, core[0], core[1], centre)
    filt(late)
    arrived(core_sem + 1, core[1] * LANES).wait_recv()
    centre = summed(late + 1, core[0], core[1], centre)
    mean[:, pl.ds(MEDGE + core[0] * LANES, core[1] * LANES)] = centre / count
    for copy in mean_copies:
        copy.wait_recv()

    total_cols = n_col * width
    span = width + 2 * MEDGE
    at = lax.broadcasted_iota(jnp.int32, (slab, span), 1) + (col * width - MEDGE)
    inside = (at >= 0) & (at < total_cols)
    line = lax.broadcasted_iota(jnp.int32, (slab, 1), 0)
    half = jnp.zeros((slab, 1), jnp.int32)
    for r in range(slab):
        half = jnp.where(line == r, widths[r], half)
    centre = jnp.where(inside, mean[...], 0.0)
    running = centre
    for j in range(1, BWMAX + 1):
        pair = pltpu.roll(centre, j, 1) + pltpu.roll(centre, span - j, 1)
        running = running + jnp.where(half >= j, pair, 0.0)
    count = jnp.minimum(at, half) + jnp.minimum(total_cols - 1 - at, half) + 1
    count = jnp.maximum(count, 1).astype(F32)
    cycle = jnp.where(inside, centre - running / count, 0.0)
    first = cycle.astype(BF16)
    rest = cycle - first.astype(F32)
    second = rest.astype(BF16)
    third = (rest - second.astype(F32)).astype(BF16)
    cyc[0:slab] = first
    cyc[slab : 2 * slab] = second
    cyc[2 * slab : 3 * slab] = third
    for n in range(parts):
        acc = jnp.zeros((3 * slab, RW), F32)
        for k in range(3):
            acc = acc + jnp.dot(
                cyc[:, pl.ds(MEDGE + RW * (n + k - 1), RW)], ramp[k], preferred_element_type=F32
            )
        kept[:, pl.ds(n * RW, RW)] = acc[0:slab] + acc[slab : 2 * slab] + acc[2 * slab : 3 * slab]

    filt(angles - 1)
    for sem in (core_sem, core_sem + 1):
        arrived(sem, core[1] * LANES).wait_send()
    for side, halo in ((0, halo_l), (1, halo_r)):
        pltpu.make_async_remote_copy(
            halo, halo, hs_sem.at[side], hr_sem.at[side, 0], device_id={"col": left}, device_id_type=MESH
        ).wait_send()
    for copy in mean_copies:
        copy.wait_send()


def subtract_kernel(part, kept, out, obuf, o_sem):
    slabs = part.shape[0]

    def put(i):
        return pltpu.make_async_copy(obuf.at[i], out.at[i], o_sem.at[i])

    def step(i, carry):
        obuf[i] = part[i] - kept[...]
        put(i).start()
        return carry

    def wait(i, carry):
        put(i).wait()
        return carry

    lax.fori_loop(0, slabs, step, 0)
    lax.fori_loop(0, slabs, wait, 0)


def on_device(projections, detector_offset, drift_offsets, drift_fractions, cycle_widths):
    angles, rows, width = projections.shape
    slab = cycle_widths.shape[0]
    slabs = rows // slab
    blocks = width // LANES
    vmem = pl.BlockSpec(memory_space=pltpu.VMEM)
    hbm = pl.BlockSpec(memory_space=pltpu.HBM)
    dma = pltpu.SemaphoreType.DMA
    given = (projections, detector_offset, drift_offsets, drift_fractions, cycle_widths)
    part, kept = pl.pallas_call(
        exchange_kernel,
        name="exchange",
        out_shape=(
            pltpu.VMEM((slabs, angles, slab, width), F32),
            pltpu.VMEM((slab, width), F32),
        ),
        in_specs=[hbm] * 5,
        out_specs=(vmem,) * 2,
        scratch_shapes=[
            pltpu.VMEM((angles, rows, width), BF16),
            pltpu.VMEM((rows, width), F32),
            pltpu.SMEM(drift_offsets.shape, jnp.int32),
            pltpu.SMEM(drift_offsets.shape, jnp.int32),
            pltpu.SMEM(cycle_widths.shape, jnp.int32),
            pltpu.VMEM((blocks, rows + 2 * MARGIN, LANES), F32),
            pltpu.VMEM((angles, rows, width + 2 * LANES), BF16),
            pltpu.VMEM((2, 3, 2 * RW, RW), BF16),
            pltpu.VMEM((angles, slabs, slab, width), BF16),
            pltpu.VMEM((slabs, slab, width), BF16),
            pltpu.VMEM((slabs, angles, slab, width), BF16),
            pltpu.VMEM((slabs, angles, slab, RW), BF16),
            pltpu.VMEM((slabs, angles, slab, RW), BF16),
            pltpu.VMEM((slab, width + 2 * MEDGE), F32),
            pltpu.VMEM((3 * slab, width + 2 * MEDGE), BF16),
            pltpu.VMEM((3, RW, RW), BF16),
            pltpu.VMEM((2, RW, RW), BF16),
            dma((3,)),
            dma((angles,)),
            dma,
            dma((angles, 2)),
            dma((angles, 2)),
            dma((angles + 2,)),
            dma((angles + 3,)),
            dma((angles + 3,)),
            dma((2,)),
            dma((2, angles)),
            dma((2,)),
            dma((2,)),
        ],
        compiler_params=pltpu.CompilerParams(
            collective_id=0, has_side_effects=True, vmem_limit_bytes=54 * 1024 * 1024
        ),
    )(*(pltpu.with_memory_space_constraint(a, pltpu.HBM) for a in given))
    filtered = pl.pallas_call(
        subtract_kernel,
        name="subtract",
        out_shape=jax.ShapeDtypeStruct((slabs, angles, slab, width), F32),
        in_specs=[vmem] * 2,
        out_specs=hbm,
        scratch_shapes=[pltpu.VMEM((slabs, angles, slab, width), F32), dma((slabs,))],
        compiler_params=pltpu.CompilerParams(vmem_limit_bytes=24 * 1024 * 1024),
    )(part, kept)
    return filtered.reshape(slabs * angles, slab, width)


def solution(mesh):
    placed = (P("ang", None, "col"), P(None, "col"), P(), P(), P("ang"))
    return jax.shard_map(
        on_device, mesh=mesh, in_specs=placed, out_specs=P(None, "ang", "col"), check_vma=False
    )
```

```python
import functools
import math

import jax
import jax.numpy as jnp
from jax import lax
from jax.experimental import pallas as pl
from jax.experimental.pallas import tpu as pltpu
from jax.sharding import PartitionSpec as P

BWMAX = 16
RW = 256
MESH = pl.DeviceIdType.MESH
F32 = jnp.float32
BF16 = jnp.bfloat16

ORDER = (10, 6, 11, 14, 9, 2, 8, 5, 15, 7, 13, 1, 4, 3, 12)
SIDE = 4
MARGIN = 8
LANES = 128
LATE = 3
AHEAD = 2
MEDGE = 384


def cubic_taps(fraction):
    t = fraction.astype(F32) / 256.0
    t2 = t * t
    t3 = t2 * t
    return (
        (-t3 + 2.0 * t2 - t) * 0.5,
        (3.0 * t3 - 5.0 * t2 + 2.0) * 0.5,
        (-3.0 * t3 + 4.0 * t2 + t) * 0.5,
        (t3 - t2) * 0.5,
    )


def ramp_tile(shift):
    rows = lax.broadcasted_iota(jnp.int32, (RW, RW), 0)
    cols = lax.broadcasted_iota(jnp.int32, (RW, RW), 1)
    n = rows - cols + shift
    odd = (n & 1) == 1
    safe = jnp.where(n == 0, 1, n).astype(F32)
    value = jnp.where(n == 0, 0.25, jnp.where(odd, -1.0 / (math.pi**2 * safe * safe), 0.0))
    return jnp.where(jnp.abs(n) <= RW, value, 0.0)


def exchange_kernel(
    proj, offset, doff_in, dfrac_in, widths_in,
    part, kept,
    pbuf, obuf, doff, dfrac, widths, padded, lev, bands, al, al_outer, sino, halo_l, halo_r, mean, cyc, ramp, ends,
    d_sem, p_sem, o_sem, es_sem, er_sem, own_sem, s_sem, r_sem, hs_sem, hr_sem, ms_sem, mr_sem,
):
    me = lax.axis_index("ang")
    col = lax.axis_index("col")
    n_col = lax.axis_size("col")
    angles, rows, width = proj.shape
    slabs, _, slab, _ = sino.shape
    blocks = width // LANES
    y, x = me // SIDE, lax.rem(me, SIDE)
    sign = 1 - 2 * lax.rem(col, 2)
    left = lax.rem(col + n_col - 1, n_col)
    right = lax.rem(col + 1, n_col)

    def partner(place):
        return lax.rem(y + SIDE + sign * (place // SIDE), SIDE) * SIDE + lax.rem(
            x + SIDE + sign * (place % SIDE), SIDE
        )

    partners = [partner(place) for place in ORDER]

    def frame_copy(a):
        return pltpu.make_async_copy(proj.at[a], pbuf.at[a], p_sem.at[a])

    drift_copies = (
        pltpu.make_async_copy(doff_in, doff, d_sem.at[0]),
        pltpu.make_async_copy(dfrac_in, dfrac, d_sem.at[1]),
        pltpu.make_async_copy(widths_in, widths, d_sem.at[2]),
    )
    for copy in drift_copies:
        copy.start()
    offset_copy = pltpu.make_async_copy(offset, obuf, o_sem)
    frame_copy(0).start()
    offset_copy.start()
    frame_copy(1).start()

    barrier = pltpu.get_barrier_semaphore()
    for to in partners:
        pl.semaphore_signal(barrier, 1, device_id={"ang": to}, device_id_type=MESH)
    for neighbour in (left, right):
        pl.semaphore_signal(barrier, 1, device_id={"col": neighbour}, device_id_type=MESH)

    zeros = jnp.zeros((blocks, MARGIN, LANES), F32)
    padded[:, 0:MARGIN, :] = zeros
    padded[:, MARGIN + rows : 2 * MARGIN + rows, :] = zeros

    def edge_copies(a):
        return (
            pltpu.make_async_remote_copy(
                lev.at[a, :, pl.ds(width, LANES)], lev.at[a, :, pl.ds(0, LANES)],
                es_sem.at[a, 0], er_sem.at[a, 0], device_id={"col": right}, device_id_type=MESH,
            ),
            pltpu.make_async_remote_copy(
                lev.at[a, :, pl.ds(LANES, LANES)], lev.at[a, :, pl.ds(LANES + width, LANES)],
                es_sem.at[a, 1], er_sem.at[a, 1], device_id={"col": left}, device_id_type=MESH,
            ),
        )

    def level(a):
        frame_copy(a).wait()
        shift = doff[0, me * angles + a]
        taps = cubic_taps(dfrac[0, me * angles + a])

        def fill(j, carry):
            at = pl.multiple_of(j * slab, slab)
            for b in range(blocks):
                lanes = pl.ds(b * LANES, LANES)
                padded[b, pl.ds(at + MARGIN, slab), :] = (
                    pbuf[a, pl.ds(at, slab), lanes].astype(F32) + obuf[pl.ds(at, slab), lanes]
                )
            return carry

        lax.fori_loop(0, slabs, fill, 0)

        def mix(j, carry):
            at = pl.multiple_of(j * slab, slab)
            base = at + (MARGIN - 1) + shift
            total = taps[0] * padded[:, pl.ds(base, slab), :]
            for k in range(1, 4):
                total = total + taps[k] * padded[:, pl.ds(base + k, slab), :]
            total = total.astype(BF16)
            for b in range(blocks):
                lev[a, pl.ds(at, slab), pl.ds((b + 1) * LANES, LANES)] = total[b]
            return carry

        lax.fori_loop(0, slabs, mix, 0)

    def rows_to(to, a, buf, piece, sem):
        lanes = pl.ds(piece[0] * LANES, piece[1] * LANES)
        return pltpu.make_async_remote_copy(
            buf.at[to, :, lanes], sino.at[me, a, :, lanes], s_sem.at[sem], r_sem.at[sem],
            device_id={"ang": to}, device_id_type=MESH,
        )

    def weights(a):
        shift = doff[1, me * angles + a]
        taps = cubic_taps(dfrac[1, me * angles + a])
        slot = lax.rem(a, 2)
        step = 64

        def build(i, carry):
            at = pl.multiple_of(i * step, step)
            index = lax.broadcasted_iota(jnp.int32, (step, RW), 0) - lax.broadcasted_iota(jnp.int32, (step, RW), 1)
            index = index + (at - LANES - shift + 1)
            value = jnp.zeros((step, RW), F32)
            for k in range(4):
                value = jnp.where(index == k, taps[k], value)
            for p in range(3):
                piece = value.astype(BF16)
                bands[slot, p, pl.ds(at, step), :] = piece
                value = value - piece.astype(F32)
            return carry

        lax.fori_loop(0, 2 * RW // step, build, 0)

    def align(a, buf, made):
        slot = lax.rem(a, 2)
        for n in made:
            window = lev[a, :, pl.ds(n * RW, 2 * RW)]
            total = jnp.dot(window, bands[slot, 2], preferred_element_type=F32)
            total = total + jnp.dot(window, bands[slot, 1], preferred_element_type=F32)
            total = total + jnp.dot(window, bands[slot, 0], preferred_element_type=F32)
            buf[:, :, pl.ds(n * RW, RW)] = total.astype(BF16).reshape(slabs, slab, RW)

    def send(a, buf, sem, gone):
        for to in partners:
            for piece in gone:
                rows_to(to, a, buf, piece, sem).start()

    def own_copy(a, buf, piece, sem):
        lanes = pl.ds(piece[0] * LANES, piece[1] * LANES)
        return pltpu.make_async_copy(buf.at[me, :, lanes], sino.at[me, a, :, lanes], own_sem.at[sem])

    def level_and_send(a):
        level(a)
        for copy in edge_copies(a):
            copy.start()

    def take_edges(a):
        for copy in edge_copies(a):
            copy.wait_recv()
        before, after = pl.ds(0, LANES), pl.ds(LANES + width, LANES)
        lev[a, :, before] = jnp.where(col > 0, lev[a, :, before].astype(F32), 0.0).astype(BF16)
        lev[a, :, after] = jnp.where(col < n_col - 1, lev[a, :, after].astype(F32), 0.0).astype(BF16)

    whole = (0, blocks)
    step = RW // LANES
    inner = (step, blocks - 2 * step)
    outer = ((0, step), (blocks - step, step))
    parts = width // RW
    rim = MEDGE // LANES
    rims = ((0, rim), (blocks - rim, rim))
    core = (rim, blocks - 2 * rim)
    late = angles - LATE
    outer_sem, core_sem = angles, angles + 1

    for copy in drift_copies:
        copy.wait()
    weights(0)
    offset_copy.wait()
    level(0)
    for a in range(2, angles):
        frame_copy(a).start()
    align(0, al.at[0], range(1, parts - 1))
    pl.semaphore_wait(barrier, slabs + 1)
    for copy in edge_copies(0):
        copy.start()
    send(0, al.at[0], 0, (inner,))
    own_copy(0, al.at[0], inner, 0).start()
    level_and_send(1)
    weights(1)
    take_edges(0)
    align(0, al_outer, (0, parts - 1))
    level_and_send(2)
    send(0, al_outer, outer_sem, outer)
    for n, piece in enumerate(outer):
        own_copy(0, al_outer, piece, angles + n).start()

    def both(a, carry):
        take_edges(a)
        align(a, al.at[a], range(parts))
        weights(a + 1)
        send(a, al.at[a], a, (whole,))
        own_copy(a, al.at[a], whole, a).start()
        level_and_send(a + AHEAD)
        return carry

    lax.fori_loop(1, late, both, 0)

    for a in range(late, angles):
        take_edges(a)
        align(a, al.at[a], range(parts))
        if a + 1 < angles:
            weights(a + 1)
        send(a, al.at[a], a, rims)
        own_copy(a, al.at[a], whole, a).start()
        if a + AHEAD < angles:
            level_and_send(a + AHEAD)

    def last_core(a, carry):
        send(a, al.at[a], core_sem + (a - late), (core,))
        return carry

    lax.fori_loop(late, angles, last_core, 0)

    for k in range(3):
        ramp[k] = ramp_tile(RW * (k - 1)).astype(BF16)

    ends[0] = jnp.where(col > 0, ramp[0], jnp.zeros((RW, RW), BF16))
    ends[1] = jnp.where(col < n_col - 1, ramp[2], jnp.zeros((RW, RW), BF16))

    def halo_copies(k):
        return (
            pltpu.make_async_remote_copy(
                sino.at[:, k, :, pl.ds(width - RW, RW)], halo_l.at[:, k], hs_sem.at[0], hr_sem.at[0, k],
                device_id={"col": right}, device_id_type=MESH,
            ),
            pltpu.make_async_remote_copy(
                sino.at[:, k, :, pl.ds(0, RW)], halo_r.at[:, k], hs_sem.at[1], hr_sem.at[1, k],
                device_id={"col": left}, device_id_type=MESH,
            ),
        )

    def arrived(sem, width):
        part_of = sino.at[pl.ds(0, slabs - 1), 0, :, pl.ds(0, width)]
        return pltpu.make_async_remote_copy(
            part_of, part_of, s_sem.at[sem], r_sem.at[sem], device_id={"ang": me}, device_id_type=MESH
        )

    def summed(k, first, number, total):
        lanes = pl.ds(first * LANES, number * LANES)
        return lax.fori_loop(0, slabs, lambda i, t: t + sino[i, k, :, lanes].astype(F32), total)

    def pass_on(k):
        for copy in halo_copies(k):
            copy.start()

    def filt(k):
        for copy in halo_copies(k):
            copy.wait_recv()
        filt_here(k)

    def filt_here(k):
        def window(m):
            if m < 0:
                return halo_l[:, k].reshape(rows, RW)
            if m == parts:
                return halo_r[:, k].reshape(rows, RW)
            return sino[:, k, :, pl.ds(m * RW, RW)].reshape(rows, RW)

        for n in range(parts):
            acc = jnp.dot(window(n), ramp[1], preferred_element_type=F32)
            acc = acc + jnp.dot(window(n - 1), ends[0] if n == 0 else ramp[0], preferred_element_type=F32)
            acc = acc + jnp.dot(
                window(n + 1), ends[1] if n == parts - 1 else ramp[2], preferred_element_type=F32
            )
            part[:, k, :, pl.ds(n * RW, RW)] = acc.reshape(slabs, slab, RW)

    own_copy(0, al.at[0], inner, 0).wait()
    for n, piece in enumerate(outer):
        own_copy(0, al_outer, piece, angles + n).wait()
    arrived(0, inner[1] * LANES).wait_recv()
    arrived(outer_sem, 2 * RW).wait_recv()
    pass_on(0)
    total = summed(0, 0, blocks, jnp.zeros((slab, width), F32))

    def middle(k, total):
        own_copy(k, al.at[k], whole, k).wait()
        arrived(k, width).wait_recv()
        pass_on(k)
        total = summed(k, 0, blocks, total)
        filt(k - 1)
        return total

    total = lax.fori_loop(1, late, middle, total)
    count = float(slabs * angles)
    sides = [total[:, first * LANES : (first + number) * LANES] for first, number in rims]
    centre = total[:, core[0] * LANES : (core[0] + core[1]) * LANES]
    for k in range(late, angles):
        own_copy(k, al.at[k], whole, k).wait()
        arrived(k, 2 * MEDGE).wait_recv()
        sides = [summed(k, first, number, side) for (first, number), side in zip(rims, sides)]
        if k < angles - 1:
            pass_on(k)
    for (first, number), side in zip(rims, sides):
        mean[:, pl.ds(MEDGE + first * LANES, number * LANES)] = side / count

    mean_copies = (
        pltpu.make_async_remote_copy(
            mean.at[:, pl.ds(width, MEDGE)], mean.at[:, pl.ds(0, MEDGE)], ms_sem.at[0], mr_sem.at[0],
            device_id={"col": right}, device_id_type=MESH,
        ),
        pltpu.make_async_remote_copy(
            mean.at[:, pl.ds(MEDGE, MEDGE)], mean.at[:, pl.ds(MEDGE + width, MEDGE)], ms_sem.at[1], mr_sem.at[1],
            device_id={"col": left}, device_id_type=MESH,
        ),
    )
    for copy in mean_copies:
        copy.start()
    pass_on(angles - 1)
    filt(late - 1)

    for a in range(angles):
        arrived(a, inner[1] * LANES if a == 0 else 2 * MEDGE if a >= late else width).wait_send()
        for copy in edge_copies(a):
            copy.wait_send()
    arrived(outer_sem, 2 * RW).wait_send()

    for n in range(LATE - 1):
        arrived(core_sem + n, core[1] * LANES).wait_recv()
        centre = summed(late + n, core[0], core[1], centre)
        filt(late + n)
    for copy in mean_copies:
        copy.wait_recv()

    total_cols = n_col * width
    line = lax.broadcasted_iota(jnp.int32, (slab, 1), 0)
    half = jnp.zeros((slab, 1), jnp.int32)
    for r in range(slab):
        half = jnp.where(line == r, widths[r], half)

    def find_cycle(first, end):
        start, stop = max(first - LANES, 0), min(end + LANES, width + 2 * MEDGE)
        span = stop - start
        at = lax.broadcasted_iota(jnp.int32, (slab, span), 1) + (col * width - MEDGE + start)
        inside = (at >= 0) & (at < total_cols)
        centre = jnp.where(inside, mean[:, pl.ds(start, span)], 0.0)
        running = centre
        for j in range(1, BWMAX + 1):
            pair = pltpu.roll(centre, j, 1) + pltpu.roll(centre, span - j, 1)
            running = running + jnp.where(half >= j, pair, 0.0)
        terms = jnp.minimum(at, half) + jnp.minimum(total_cols - 1 - at, half) + 1
        terms = jnp.maximum(terms, 1).astype(F32)
        rest = jnp.where(inside, centre - running / terms, 0.0)[:, first - start : end - start]
        for p in range(3):
            piece = rest.astype(BF16)
            cyc[p * slab : (p + 1) * slab, pl.ds(first, end - first)] = piece
            rest = rest - piece.astype(F32)

    inner_first = MEDGE + (core[0] - 1) * LANES
    inner_end = MEDGE + (core[0] + core[1] + 1) * LANES
    find_cycle(0, inner_first)
    find_cycle(inner_end, width + 2 * MEDGE)
    arrived(core_sem + LATE - 1, core[1] * LANES).wait_recv()
    for copy in halo_copies(angles - 1):
        copy.wait_recv()
    centre = summed(angles - 1, core[0], core[1], centre)
    mean[:, pl.ds(MEDGE + core[0] * LANES, core[1] * LANES)] = centre / count
    filt_here(angles - 1)
    find_cycle(inner_first, inner_end)
    for n in range(parts):
        acc = jnp.zeros((3 * slab, RW), F32)
        for k in range(3):
            acc = acc + jnp.dot(
                cyc[:, pl.ds(MEDGE + RW * (n + k - 1), RW)], ramp[k], preferred_element_type=F32
            )
        kept[:, pl.ds(n * RW, RW)] = acc[0:slab] + acc[slab : 2 * slab] + acc[2 * slab : 3 * slab]

    for sem in range(core_sem, core_sem + LATE):
        arrived(sem, core[1] * LANES).wait_send()
    for side, halo in ((0, halo_l), (1, halo_r)):
        pltpu.make_async_remote_copy(
            halo, halo, hs_sem.at[side], hr_sem.at[side, 0], device_id={"col": left}, device_id_type=MESH
        ).wait_send()
    for copy in mean_copies:
        copy.wait_send()


def subtract_kernel(part, kept, out, obuf, o_sem):
    steps = o_sem.shape[0]
    group = part.shape[0] // steps

    def put(i):
        some = pl.ds(i * group, group)
        return pltpu.make_async_copy(obuf.at[some], out.at[some], o_sem.at[i])

    def step(i, carry):
        some = pl.ds(i * group, group)
        obuf[some] = part[some] - kept[...]
        put(i).start()
        return carry

    def wait(i, carry):
        put(i).wait()
        return carry

    lax.fori_loop(0, steps, step, 0)
    lax.fori_loop(0, steps, wait, 0)


def on_device(projections, detector_offset, drift_offsets, drift_fractions, cycle_widths):
    angles, rows, width = projections.shape
    slab = cycle_widths.shape[0]
    slabs = rows // slab
    blocks = width // LANES
    vmem = pl.BlockSpec(memory_space=pltpu.VMEM)
    hbm = pl.BlockSpec(memory_space=pltpu.HBM)
    dma = pltpu.SemaphoreType.DMA
    given = (projections, detector_offset, drift_offsets, drift_fractions, cycle_widths)
    part, kept = pl.pallas_call(
        exchange_kernel,
        name="exchange",
        out_shape=(
            pltpu.VMEM((slabs, angles, slab, width), F32),
            pltpu.VMEM((slab, width), F32),
        ),
        in_specs=[hbm] * 5,
        out_specs=(vmem,) * 2,
        scratch_shapes=[
            pltpu.VMEM((angles, rows, width), BF16),
            pltpu.VMEM((rows, width), F32),
            pltpu.SMEM(drift_offsets.shape, jnp.int32),
            pltpu.SMEM(drift_offsets.shape, jnp.int32),
            pltpu.SMEM(cycle_widths.shape, jnp.int32),
            pltpu.VMEM((blocks, rows + 2 * MARGIN, LANES), F32),
            pltpu.VMEM((angles, rows, width + 2 * LANES), BF16),
            pltpu.VMEM((2, 3, 2 * RW, RW), BF16),
            pltpu.VMEM((angles, slabs, slab, width), BF16),
            pltpu.VMEM((slabs, slab, width), BF16),
            pltpu.VMEM((slabs, angles, slab, width), BF16),
            pltpu.VMEM((slabs, angles, slab, RW), BF16),
            pltpu.VMEM((slabs, angles, slab, RW), BF16),
            pltpu.VMEM((slab, width + 2 * MEDGE), F32),
            pltpu.VMEM((3 * slab, width + 2 * MEDGE), BF16),
            pltpu.VMEM((3, RW, RW), BF16),
            pltpu.VMEM((2, RW, RW), BF16),
            dma((3,)),
            dma((angles,)),
            dma,
            dma((angles, 2)),
            dma((angles, 2)),
            dma((angles + 2,)),
            dma((angles + 1 + LATE,)),
            dma((angles + 1 + LATE,)),
            dma((2,)),
            dma((2, angles)),
            dma((2,)),
            dma((2,)),
        ],
        compiler_params=pltpu.CompilerParams(
            collective_id=0, has_side_effects=True, vmem_limit_bytes=54 * 1024 * 1024
        ),
    )(*(pltpu.with_memory_space_constraint(a, pltpu.HBM) for a in given))
    frames = (slabs * angles, slab, width)
    return pl.pallas_call(
        subtract_kernel,
        name="subtract",
        out_shape=jax.ShapeDtypeStruct(frames, F32),
        in_specs=[vmem] * 2,
        out_specs=hbm,
        scratch_shapes=[pltpu.VMEM(frames, F32), dma((slabs,))],
        compiler_params=pltpu.CompilerParams(vmem_limit_bytes=24 * 1024 * 1024),
    )(part.reshape(frames), kept)


def solution(mesh):
    placed = (P("ang", None, "col"), P(None, "col"), P(), P(), P("ang"))
    return jax.shard_map(
        on_device, mesh=mesh, in_specs=placed, out_specs=P(None, "ang", "col"), check_vma=False
    )
```

```python
import functools
import math

import jax
import jax.numpy as jnp
from jax import lax
from jax.experimental import pallas as pl
from jax.experimental.pallas import tpu as pltpu
from jax.sharding import PartitionSpec as P

BWMAX = 16
RW = 256
MESH = pl.DeviceIdType.MESH
F32 = jnp.float32
BF16 = jnp.bfloat16

ORDER = (10, 6, 11, 14, 9, 2, 8, 5, 15, 7, 13, 1, 4, 3, 12)
SIDE = 4
MARGIN = 8
LANES = 128
LATE = 3
AHEAD = 2
MEDGE = 384


def cubic_taps(fraction):
    t = fraction.astype(F32) / 256.0
    t2 = t * t
    t3 = t2 * t
    return (
        (-t3 + 2.0 * t2 - t) * 0.5,
        (3.0 * t3 - 5.0 * t2 + 2.0) * 0.5,
        (-3.0 * t3 + 4.0 * t2 + t) * 0.5,
        (t3 - t2) * 0.5,
    )


def ramp_tile(shift):
    rows = lax.broadcasted_iota(jnp.int32, (RW, RW), 0)
    cols = lax.broadcasted_iota(jnp.int32, (RW, RW), 1)
    n = rows - cols + shift
    odd = (n & 1) == 1
    safe = jnp.where(n == 0, 1, n).astype(F32)
    value = jnp.where(n == 0, 0.25, jnp.where(odd, -1.0 / (math.pi**2 * safe * safe), 0.0))
    return jnp.where(jnp.abs(n) <= RW, value, 0.0)


def exchange_kernel(
    proj, offset, doff_in, dfrac_in, widths_in,
    part, kept,
    pbuf, obuf, doff, dfrac, widths, padded, lev, bands, al, al_outer, sino, halo_l, halo_r, mean, cyc, ramp, ends,
    d_sem, p_sem, o_sem, es_sem, er_sem, own_sem, s_sem, r_sem, hs_sem, hr_sem, ms_sem, mr_sem,
):
    me = lax.axis_index("ang")
    col = lax.axis_index("col")
    n_col = lax.axis_size("col")
    angles, rows, width = proj.shape
    slabs, _, slab, _ = sino.shape
    blocks = width // LANES
    y, x = me // SIDE, lax.rem(me, SIDE)
    sign = 1 - 2 * lax.rem(col, 2)
    left = lax.rem(col + n_col - 1, n_col)
    right = lax.rem(col + 1, n_col)

    def partner(place):
        return lax.rem(y + SIDE + sign * (place // SIDE), SIDE) * SIDE + lax.rem(
            x + SIDE + sign * (place % SIDE), SIDE
        )

    partners = [partner(place) for place in ORDER]

    def frame_copy(a):
        return pltpu.make_async_copy(proj.at[a], pbuf.at[a], p_sem.at[a])

    drift_copies = (
        pltpu.make_async_copy(doff_in, doff, d_sem.at[0]),
        pltpu.make_async_copy(dfrac_in, dfrac, d_sem.at[1]),
        pltpu.make_async_copy(widths_in, widths, d_sem.at[2]),
    )
    for copy in drift_copies:
        copy.start()
    offset_copy = pltpu.make_async_copy(offset, obuf, o_sem)
    frame_copy(0).start()
    offset_copy.start()
    frame_copy(1).start()

    barrier = pltpu.get_barrier_semaphore()
    for to in partners:
        pl.semaphore_signal(barrier, 1, device_id={"ang": to}, device_id_type=MESH)
    for neighbour in (left, right):
        pl.semaphore_signal(barrier, 1, device_id={"col": neighbour}, device_id_type=MESH)

    zeros = jnp.zeros((blocks, MARGIN, LANES), F32)
    padded[:, 0:MARGIN, :] = zeros
    padded[:, MARGIN + rows : 2 * MARGIN + rows, :] = zeros

    def edge_copies(a):
        return (
            pltpu.make_async_remote_copy(
                lev.at[a, :, pl.ds(width, LANES)], lev.at[a, :, pl.ds(0, LANES)],
                es_sem.at[a, 0], er_sem.at[a, 0], device_id={"col": right}, device_id_type=MESH,
            ),
            pltpu.make_async_remote_copy(
                lev.at[a, :, pl.ds(LANES, LANES)], lev.at[a, :, pl.ds(LANES + width, LANES)],
                es_sem.at[a, 1], er_sem.at[a, 1], device_id={"col": left}, device_id_type=MESH,
            ),
        )

    def level(a):
        frame_copy(a).wait()
        shift = doff[0, me * angles + a]
        taps = cubic_taps(dfrac[0, me * angles + a])

        def fill(j, carry):
            at = pl.multiple_of(j * slab, slab)
            for b in range(blocks):
                lanes = pl.ds(b * LANES, LANES)
                padded[b, pl.ds(at + MARGIN, slab), :] = (
                    pbuf[a, pl.ds(at, slab), lanes].astype(F32) + obuf[pl.ds(at, slab), lanes]
                )
            return carry

        lax.fori_loop(0, slabs, fill, 0)

        def mix(j, carry):
            at = pl.multiple_of(j * slab, slab)
            base = at + (MARGIN - 1) + shift
            total = taps[0] * padded[:, pl.ds(base, slab), :]
            for k in range(1, 4):
                total = total + taps[k] * padded[:, pl.ds(base + k, slab), :]
            total = total.astype(BF16)
            for b in range(blocks):
                lev[a, pl.ds(at, slab), pl.ds((b + 1) * LANES, LANES)] = total[b]
            return carry

        lax.fori_loop(0, slabs, mix, 0)

    def rows_to(to, a, buf, piece, sem):
        lanes = pl.ds(piece[0] * LANES, piece[1] * LANES)
        return pltpu.make_async_remote_copy(
            buf.at[to, :, lanes], sino.at[me, a, :, lanes], s_sem.at[sem], r_sem.at[sem],
            device_id={"ang": to}, device_id_type=MESH,
        )

    def weights(a):
        shift = doff[1, me * angles + a]
        taps = cubic_taps(dfrac[1, me * angles + a])
        slot = lax.rem(a, 2)
        step = 64

        def build(i, carry):
            at = pl.multiple_of(i * step, step)
            index = lax.broadcasted_iota(jnp.int32, (step, RW), 0) - lax.broadcasted_iota(jnp.int32, (step, RW), 1)
            index = index + (at - LANES - shift + 1)
            value = jnp.zeros((step, RW), F32)
            for k in range(4):
                value = jnp.where(index == k, taps[k], value)
            for p in range(3):
                piece = value.astype(BF16)
                bands[slot, p, pl.ds(at, step), :] = piece
                value = value - piece.astype(F32)
            return carry

        lax.fori_loop(0, 2 * RW // step, build, 0)

    def align(a, buf, made):
        slot = lax.rem(a, 2)
        for n in made:
            window = lev[a, :, pl.ds(n * RW, 2 * RW)]
            total = jnp.dot(window, bands[slot, 2], preferred_element_type=F32)
            total = total + jnp.dot(window, bands[slot, 1], preferred_element_type=F32)
            total = total + jnp.dot(window, bands[slot, 0], preferred_element_type=F32)
            buf[:, :, pl.ds(n * RW, RW)] = total.astype(BF16).reshape(slabs, slab, RW)

    def send(a, buf, sem, gone):
        for to in partners:
            for piece in gone:
                rows_to(to, a, buf, piece, sem).start()

    def own_copy(a, buf, piece, sem):
        lanes = pl.ds(piece[0] * LANES, piece[1] * LANES)
        return pltpu.make_async_copy(buf.at[me, :, lanes], sino.at[me, a, :, lanes], own_sem.at[sem])

    def level_and_send(a):
        level(a)
        for copy in edge_copies(a):
            copy.start()

    def take_edges(a):
        for copy in edge_copies(a):
            copy.wait_recv()
        before, after = pl.ds(0, LANES), pl.ds(LANES + width, LANES)
        lev[a, :, before] = jnp.where(col > 0, lev[a, :, before].astype(F32), 0.0).astype(BF16)
        lev[a, :, after] = jnp.where(col < n_col - 1, lev[a, :, after].astype(F32), 0.0).astype(BF16)

    whole = (0, blocks)
    step = RW // LANES
    inner = (step, blocks - 2 * step)
    outer = ((0, step), (blocks - step, step))
    parts = width // RW
    rim = MEDGE // LANES
    rims = ((0, rim), (blocks - rim, rim))
    core = (rim, blocks - 2 * rim)
    late = angles - LATE
    outer_sem, core_sem = angles, angles + 1

    for copy in drift_copies:
        copy.wait()
    weights(0)
    offset_copy.wait()
    level(0)
    for a in range(2, angles):
        frame_copy(a).start()
    align(0, al.at[0], range(1, parts - 1))
    pl.semaphore_wait(barrier, slabs + 1)
    for copy in edge_copies(0):
        copy.start()
    send(0, al.at[0], 0, (inner,))
    own_copy(0, al.at[0], inner, 0).start()
    level_and_send(1)
    weights(1)
    take_edges(0)
    align(0, al_outer, (0, parts - 1))
    level_and_send(2)
    send(0, al_outer, outer_sem, outer)
    for n, piece in enumerate(outer):
        own_copy(0, al_outer, piece, angles + n).start()

    def both(a, carry):
        take_edges(a)
        align(a, al.at[a], range(parts))
        weights(a + 1)
        send(a, al.at[a], a, (whole,))
        own_copy(a, al.at[a], whole, a).start()
        level_and_send(a + AHEAD)
        return carry

    lax.fori_loop(1, late, both, 0)

    for a in range(late, angles):
        take_edges(a)
        align(a, al.at[a], range(parts))
        if a + 1 < angles:
            weights(a + 1)
        send(a, al.at[a], a, rims)
        own_copy(a, al.at[a], whole, a).start()
        if a + AHEAD < angles:
            level_and_send(a + AHEAD)

    def last_core(a, carry):
        send(a, al.at[a], core_sem + (a - late), (core,))
        return carry

    lax.fori_loop(late, angles, last_core, 0)

    for k in range(3):
        ramp[k] = ramp_tile(RW * (k - 1)).astype(BF16)

    ends[0] = jnp.where(col > 0, ramp[0], jnp.zeros((RW, RW), BF16))
    ends[1] = jnp.where(col < n_col - 1, ramp[2], jnp.zeros((RW, RW), BF16))

    def halo_copies(k):
        return (
            pltpu.make_async_remote_copy(
                sino.at[:, k, :, pl.ds(width - RW, RW)], halo_l.at[:, k], hs_sem.at[0], hr_sem.at[0, k],
                device_id={"col": right}, device_id_type=MESH,
            ),
            pltpu.make_async_remote_copy(
                sino.at[:, k, :, pl.ds(0, RW)], halo_r.at[:, k], hs_sem.at[1], hr_sem.at[1, k],
                device_id={"col": left}, device_id_type=MESH,
            ),
        )

    def arrived(sem, width):
        part_of = sino.at[pl.ds(0, slabs - 1), 0, :, pl.ds(0, width)]
        return pltpu.make_async_remote_copy(
            part_of, part_of, s_sem.at[sem], r_sem.at[sem], device_id={"ang": me}, device_id_type=MESH
        )

    def summed(k, first, number, total):
        lanes = pl.ds(first * LANES, number * LANES)
        return lax.fori_loop(0, slabs, lambda i, t: t + sino[i, k, :, lanes].astype(F32), total)

    def pass_on(k):
        for copy in halo_copies(k):
            copy.start()

    def filt(k):
        for copy in halo_copies(k):
            copy.wait_recv()
        filt_here(k, range(-1, parts + 1), False)

    def filt_here(k, windows, add):
        def window(m):
            if m < 0:
                return halo_l[:, k].reshape(rows, RW)
            if m == parts:
                return halo_r[:, k].reshape(rows, RW)
            return sino[:, k, :, pl.ds(m * RW, RW)].reshape(rows, RW)

        for n in range(parts):
            acc = None
            for m in (n, n - 1, n + 1):
                if m not in windows:
                    continue
                taps = ends[0] if m < 0 else ends[1] if m == parts else ramp[m - n + 1]
                term = jnp.dot(window(m), taps, preferred_element_type=F32)
                acc = term if acc is None else acc + term
            lanes = pl.ds(n * RW, RW)
            acc = acc.reshape(slabs, slab, RW)
            part[:, k, :, lanes] = part[:, k, :, lanes] + acc if add else acc

    own_copy(0, al.at[0], inner, 0).wait()
    for n, piece in enumerate(outer):
        own_copy(0, al_outer, piece, angles + n).wait()
    arrived(0, inner[1] * LANES).wait_recv()
    arrived(outer_sem, 2 * RW).wait_recv()
    pass_on(0)
    total = summed(0, 0, blocks, jnp.zeros((slab, width), F32))

    def middle(k, total):
        own_copy(k, al.at[k], whole, k).wait()
        arrived(k, width).wait_recv()
        pass_on(k)
        total = summed(k, 0, blocks, total)
        filt(k - 1)
        return total

    total = lax.fori_loop(1, late, middle, total)
    count = float(slabs * angles)
    sides = [total[:, first * LANES : (first + number) * LANES] for first, number in rims]
    centre = total[:, core[0] * LANES : (core[0] + core[1]) * LANES]
    for k in range(late, angles):
        own_copy(k, al.at[k], whole, k).wait()
        arrived(k, 2 * MEDGE).wait_recv()
        sides = [summed(k, first, number, side) for (first, number), side in zip(rims, sides)]
        if k < angles - 1:
            pass_on(k)
    for (first, number), side in zip(rims, sides):
        mean[:, pl.ds(MEDGE + first * LANES, number * LANES)] = side / count

    mean_copies = (
        pltpu.make_async_remote_copy(
            mean.at[:, pl.ds(width, MEDGE)], mean.at[:, pl.ds(0, MEDGE)], ms_sem.at[0], mr_sem.at[0],
            device_id={"col": right}, device_id_type=MESH,
        ),
        pltpu.make_async_remote_copy(
            mean.at[:, pl.ds(MEDGE, MEDGE)], mean.at[:, pl.ds(MEDGE + width, MEDGE)], ms_sem.at[1], mr_sem.at[1],
            device_id={"col": left}, device_id_type=MESH,
        ),
    )
    for copy in mean_copies:
        copy.start()
    pass_on(angles - 1)
    filt(late - 1)

    for a in range(angles):
        arrived(a, inner[1] * LANES if a == 0 else 2 * MEDGE if a >= late else width).wait_send()
        for copy in edge_copies(a):
            copy.wait_send()
    arrived(outer_sem, 2 * RW).wait_send()

    for n in range(LATE - 1):
        arrived(core_sem + n, core[1] * LANES).wait_recv()
        centre = summed(late + n, core[0], core[1], centre)
        filt(late + n)
    for copy in mean_copies:
        copy.wait_recv()

    total_cols = n_col * width
    line = lax.broadcasted_iota(jnp.int32, (slab, 1), 0)
    half = jnp.zeros((slab, 1), jnp.int32)
    for r in range(slab):
        half = jnp.where(line == r, widths[r], half)

    def find_cycle(first, end):
        start, stop = max(first - LANES, 0), min(end + LANES, width + 2 * MEDGE)
        span = stop - start
        at = lax.broadcasted_iota(jnp.int32, (slab, span), 1) + (col * width - MEDGE + start)
        inside = (at >= 0) & (at < total_cols)
        centre = jnp.where(inside, mean[:, pl.ds(start, span)], 0.0)
        running = centre
        for j in range(1, BWMAX + 1):
            pair = pltpu.roll(centre, j, 1) + pltpu.roll(centre, span - j, 1)
            running = running + jnp.where(half >= j, pair, 0.0)
        terms = jnp.minimum(at, half) + jnp.minimum(total_cols - 1 - at, half) + 1
        terms = jnp.maximum(terms, 1).astype(F32)
        rest = jnp.where(inside, centre - running / terms, 0.0)[:, first - start : end - start]
        for p in range(3):
            piece = rest.astype(BF16)
            cyc[p * slab : (p + 1) * slab, pl.ds(first, end - first)] = piece
            rest = rest - piece.astype(F32)

    inner_first = MEDGE + (core[0] - 1) * LANES
    inner_end = MEDGE + (core[0] + core[1] + 1) * LANES
    find_cycle(0, inner_first)
    find_cycle(inner_end, width + 2 * MEDGE)
    for copy in halo_copies(angles - 1):
        copy.wait_recv()
    filt_here(angles - 1, (-1, 0, parts - 1, parts), False)
    arrived(core_sem + LATE - 1, core[1] * LANES).wait_recv()
    centre = summed(angles - 1, core[0], core[1], centre)
    mean[:, pl.ds(MEDGE + core[0] * LANES, core[1] * LANES)] = centre / count
    filt_here(angles - 1, range(1, parts - 1), True)
    find_cycle(inner_first, inner_end)
    for n in range(parts):
        acc = jnp.zeros((3 * slab, RW), F32)
        for k in range(3):
            acc = acc + jnp.dot(
                cyc[:, pl.ds(MEDGE + RW * (n + k - 1), RW)], ramp[k], preferred_element_type=F32
            )
        kept[:, pl.ds(n * RW, RW)] = acc[0:slab] + acc[slab : 2 * slab] + acc[2 * slab : 3 * slab]

    for sem in range(core_sem, core_sem + LATE):
        arrived(sem, core[1] * LANES).wait_send()
    for side, halo in ((0, halo_l), (1, halo_r)):
        pltpu.make_async_remote_copy(
            halo, halo, hs_sem.at[side], hr_sem.at[side, 0], device_id={"col": left}, device_id_type=MESH
        ).wait_send()
    for copy in mean_copies:
        copy.wait_send()


def subtract_kernel(part, kept, out, obuf, o_sem):
    steps = o_sem.shape[0]
    group = part.shape[0] // steps

    def put(i):
        some = pl.ds(i * group, group)
        return pltpu.make_async_copy(obuf.at[some], out.at[some], o_sem.at[i])

    def step(i, carry):
        some = pl.ds(i * group, group)
        obuf[some] = part[some] - kept[...]
        put(i).start()
        return carry

    def wait(i, carry):
        put(i).wait()
        return carry

    lax.fori_loop(0, steps, step, 0)
    lax.fori_loop(0, steps, wait, 0)


def on_device(projections, detector_offset, drift_offsets, drift_fractions, cycle_widths):
    angles, rows, width = projections.shape
    slab = cycle_widths.shape[0]
    slabs = rows // slab
    blocks = width // LANES
    vmem = pl.BlockSpec(memory_space=pltpu.VMEM)
    hbm = pl.BlockSpec(memory_space=pltpu.HBM)
    dma = pltpu.SemaphoreType.DMA
    given = (projections, detector_offset, drift_offsets, drift_fractions, cycle_widths)
    part, kept = pl.pallas_call(
        exchange_kernel,
        name="exchange",
        out_shape=(
            pltpu.VMEM((slabs, angles, slab, width), F32),
            pltpu.VMEM((slab, width), F32),
        ),
        in_specs=[hbm] * 5,
        out_specs=(vmem,) * 2,
        scratch_shapes=[
            pltpu.VMEM((angles, rows, width), BF16),
            pltpu.VMEM((rows, width), F32),
            pltpu.SMEM(drift_offsets.shape, jnp.int32),
            pltpu.SMEM(drift_offsets.shape, jnp.int32),
            pltpu.SMEM(cycle_widths.shape, jnp.int32),
            pltpu.VMEM((blocks, rows + 2 * MARGIN, LANES), F32),
            pltpu.VMEM((angles, rows, width + 2 * LANES), BF16),
            pltpu.VMEM((2, 3, 2 * RW, RW), BF16),
            pltpu.VMEM((angles, slabs, slab, width), BF16),
            pltpu.VMEM((slabs, slab, width), BF16),
            pltpu.VMEM((slabs, angles, slab, width), BF16),
            pltpu.VMEM((slabs, angles, slab, RW), BF16),
            pltpu.VMEM((slabs, angles, slab, RW), BF16),
            pltpu.VMEM((slab, width + 2 * MEDGE), F32),
            pltpu.VMEM((3 * slab, width + 2 * MEDGE), BF16),
            pltpu.VMEM((3, RW, RW), BF16),
            pltpu.VMEM((2, RW, RW), BF16),
            dma((3,)),
            dma((angles,)),
            dma,
            dma((angles, 2)),
            dma((angles, 2)),
            dma((angles + 2,)),
            dma((angles + 1 + LATE,)),
            dma((angles + 1 + LATE,)),
            dma((2,)),
            dma((2, angles)),
            dma((2,)),
            dma((2,)),
        ],
        compiler_params=pltpu.CompilerParams(
            collective_id=0, has_side_effects=True, vmem_limit_bytes=54 * 1024 * 1024
        ),
    )(*(pltpu.with_memory_space_constraint(a, pltpu.HBM) for a in given))
    frames = (slabs * angles, slab, width)
    return pl.pallas_call(
        subtract_kernel,
        name="subtract",
        out_shape=jax.ShapeDtypeStruct(frames, F32),
        in_specs=[vmem] * 2,
        out_specs=hbm,
        scratch_shapes=[pltpu.VMEM(frames, F32), dma((slabs,))],
        compiler_params=pltpu.CompilerParams(vmem_limit_bytes=24 * 1024 * 1024),
    )(part.reshape(frames), kept)


def solution(mesh):
    placed = (P("ang", None, "col"), P(None, "col"), P(), P(), P("ang"))
    return jax.shard_map(
        on_device, mesh=mesh, in_specs=placed, out_specs=P(None, "ang", "col"), check_vma=False
    )
```
